1024 devices in a mesh: energy: 32 (over z, y_lo), rows: 32 (over y_hi, x, core).
Axes of the slice: x: 8, y: 8 (y_hi: 2, y_lo: 4; y = y_hi * 4 + y_lo), z: 8, core: 2. Of those that a mesh axis runs over, the one named last changes fastest.
Arguments:
- green_window: bfloat16 [2, 2, 64, 32, 9216], P(None, None, 'energy', 'rows'), may hold values from -6 to 6
- screened: bfloat16 [2, 2, 64, 32, 9216], P(None, None, None, 'rows', 'energy'), may hold values from -6 to 6
- retarded: bfloat16 [2, 64, 32, 3, 96, 192], P(None, 'energy', 'rows'), may hold values from -0.375 to 0.375
- energy_order: int32 [64], replicated, may hold values from 0 to 63, each once
- window_start: int32 [32], P('rows'), may hold values from 0 to 96
Outputs:
- density: float32 [2, 2, 64, 32, 192], P(None, None, 'energy', 'rows')
The draws below stay inside these ranges and needn't reach their ends.
Inputs may be any that keep to these rules, and one draw needn't show every extreme that they name: A permutation of the energy indices: slot s holds energy energy_order[s]. Block row i's window covers its orbitals window_start[i] to window_start[i] + 95.
All inputs are finite; a program needn't handle non-finite values.
Results may differ from the reference program's by a relative error of at most 0.0029.
Values may be sent and summed in bfloat16 or wider, within the bound.
A program may use at most 32 MiB of HBM per device.

```python
import jax
import jax.numpy as jnp
from jax import lax

B = 192
SLAB = 96
NE = 64
NB = 32


def with_ends(values, rng, least, largest):
    shape = values.shape
    spot = [jax.random.randint(jax.random.fold_in(rng, axis), (), 0, shape[axis]) for axis in range(len(shape))]
    values = values.at[tuple(spot)].set(least)
    longest = shape.index(max(shape))
    spot[longest] = (spot[longest] + 1) % shape[longest]
    return values.at[tuple(spot)].set(largest)


def block_levels(rng, extent, pieces, least, top_value):
    level = 1.0
    for axis_at, parts in pieces:
        draws = jax.random.uniform(jax.random.fold_in(jax.random.fold_in(rng, 6), axis_at), (parts,), jnp.float32, least / len(pieces), top_value / len(pieces))
        level = level * jnp.repeat(jnp.exp(draws), extent[axis_at] // parts).reshape((-1,) + (1,) * (len(extent) - 1 - axis_at))
    return level


def bell_draw(key, dims, scale, limit, cuts=(), kind=jnp.bfloat16):
    gain = block_levels(key, dims, cuts, -0.22, 0.18) if cuts else 1.0
    array = jax.random.normal(key, dims, jnp.float32) * scale * gain
    return jnp.minimum(jnp.maximum(array, -limit), limit).astype(kind)


def setup_inputs(seed: int = 0) -> dict:
    keys = jax.random.split(jax.random.key(seed), 6)
    return {
        "green_window": bell_draw(keys[0], (2, 2, NE, NB, SLAB * SLAB), 1.0, 6.0, ((2, 32), (3, 32))),
        "screened": bell_draw(keys[1], (2, 2, NE, NB, SLAB * SLAB), 1.0, 6.0, ((3, 32), (4, 32))),
        "retarded": bell_draw(keys[2], (2, NE, NB, 3, SLAB, B), (3 * SLAB) ** -0.5, 0.375, ((1, 32), (2, 32))),
        "energy_order": jax.random.permutation(keys[3], NE).astype(jnp.int32),
        "window_start": with_ends(jax.random.randint(keys[4], (NB,), 0, B - SLAB + 1), jax.random.fold_in(keys[4], 1), 0, B - SLAB).astype(jnp.int32),
    }


def convolve_row(green_row, screen_row):
    green_complex = lax.complex(green_row[:, 0], green_row[:, 1])
    screen_complex = lax.complex(screen_row[:, 0], screen_row[:, 1])
    times = jnp.fft.fft(green_complex, axis=1)
    result = 1j * jnp.fft.ifft(times * screen_complex, axis=1)
    return jnp.stack([jnp.real(result), jnp.imag(result)], axis=1).astype(jnp.bfloat16)


def reference(green_window, screened, retarded, energy_order, window_start):
    inverse = jnp.argsort(energy_order).astype(jnp.int32)
    order = energy_order.astype(jnp.int32)
    block_count = green_window.shape[3]

    def one_row(row):
        green_row = lax.dynamic_index_in_dim(green_window, row, 3, keepdims=False)
        green_row = jnp.take(green_row, inverse, axis=2).astype(jnp.float32)
        screen_row = lax.dynamic_index_in_dim(screened, row, 3, keepdims=False).astype(jnp.float32)
        sigma_true = convolve_row(green_row, screen_row)
        return jnp.take(sigma_true, order, axis=2)

    sigma_rows = lax.map(one_row, jnp.arange(block_count, dtype=jnp.int32))
    zero_row = jnp.zeros_like(sigma_rows[:1])
    padded = jnp.concatenate([zero_row, sigma_rows, zero_row], axis=0)

    def density_row(row):
        nearby = lax.dynamic_slice_in_dim(padded, row, 3, 0).astype(jnp.float32)
        nearby = nearby.reshape(3, 2, 2, NE, SLAB, SLAB)
        coupling = lax.dynamic_index_in_dim(retarded, row, 2, keepdims=False).astype(jnp.float32)
        dens_re = jnp.zeros((2, NE, B), jnp.float32)
        dens_im = jnp.zeros((2, NE, B), jnp.float32)
        for neighbour in range(3):
            part_re = nearby[neighbour, :, 0]
            part_im = nearby[neighbour, :, 1]
            right_re = coupling[0, :, neighbour]
            right_im = coupling[1, :, neighbour]
            inner_re = jnp.einsum("gepq,epa->geqa", part_re, right_re) - jnp.einsum("gepq,epa->geqa", part_im, right_im)
            inner_im = jnp.einsum("gepq,epa->geqa", part_re, right_im) + jnp.einsum("gepq,epa->geqa", part_im, right_re)
            dens_re = dens_re + jnp.sum(inner_re * right_re[None] + inner_im * right_im[None], axis=2)
            dens_im = dens_im + jnp.sum(inner_im * right_re[None] - inner_re * right_im[None], axis=2)
        own = nearby[1]
        diagonal_part = jnp.diagonal(own, axis1=3, axis2=4)
        start = window_start[row]
        column_ids = lax.broadcasted_iota(jnp.int32, (SLAB, B), 1)
        window_ids = lax.broadcasted_iota(jnp.int32, (SLAB, B), 0)
        place = (column_ids == window_ids + start).astype(jnp.float32)
        direct = jnp.einsum("gcep,pa->gcea", diagonal_part, place, precision=lax.Precision.HIGHEST)
        return jnp.stack([dens_re, dens_im], axis=1) + direct

    result = lax.map(density_row, jnp.arange(block_count, dtype=jnp.int32))
    return jnp.transpose(result, (1, 2, 3, 0, 4))
```

```python
import functools
import math

import jax
import jax.numpy as jnp
import numpy as np
from jax import lax
from jax.experimental import pallas as pl
from jax.experimental.pallas import tpu as pltpu
from jax.sharding import PartitionSpec as P

MESH = pl.DeviceIdType.MESH
LANES = 128


def phase_tables(total):
    turns = np.outer(np.arange(total), np.arange(total)) % total
    angle = 2.0 * math.pi / total * turns
    parts = []
    for exact in (np.cos(angle), np.sin(angle)):
        high = exact.astype(jnp.bfloat16)
        low = (exact - high.astype(np.float64)).astype(jnp.bfloat16)
        parts.append((high, low))
    stacked = np.stack([parts[0][0], parts[1][0], parts[0][1], parts[1][1]])
    return np.tile(stacked, (1, 1, 4))


def dot(left, right):
    return jnp.dot(left, right, preferred_element_type=jnp.float32)


def iota(shape, axis):
    return lax.broadcasted_iota(jnp.int32, shape, axis)


def kernel(
    green, screened, retarded, order, start, tables, out,
    green_v, screen_v, own_v, order_v, start_v, tables_v,
    flat, chunks, land_one, weights, forward, backward,
    chunks_two, land_two, rows_two, from_left, from_right, right_side, spread, halo_out, halo_in,
    local_sem, send_one, recv_one, send_two, recv_two, ret_send, ret_recv, halo_send, halo_recv,
):
    n_e = lax.axis_size("energy")
    n_r = lax.axis_size("rows")
    me = lax.axis_index("energy")
    row = lax.axis_index("rows")
    slab, width = own_v.shape[2], own_v.shape[3]
    total = order_v.shape[1]
    per = slab // n_e
    has_left = row > 0
    has_right = row < n_r - 1

    barrier = pltpu.get_barrier_semaphore()

    @pl.loop(1, n_e)
    def _(step):
        pl.semaphore_signal(
            barrier, inc=1, device_id={"energy": lax.rem(me + step, n_e)}, device_id_type=MESH
        )

    @pl.when(has_left)
    def _():
        pl.semaphore_signal(barrier, inc=1, device_id={"rows": row - 1}, device_id_type=MESH)

    @pl.when(has_right)
    def _():
        pl.semaphore_signal(barrier, inc=1, device_id={"rows": row + 1}, device_id_type=MESH)

    loads = [
        pltpu.make_async_copy(green, green_v, local_sem.at[0]),
        pltpu.make_async_copy(order, order_v, local_sem.at[1]),
        pltpu.make_async_copy(tables, tables_v, local_sem.at[2]),
        pltpu.make_async_copy(screened, screen_v, local_sem.at[3]),
        pltpu.make_async_copy(retarded.at[:, :, 1], own_v, local_sem.at[4]),
        pltpu.make_async_copy(start, start_v, local_sem.at[5]),
    ]
    for load in loads:
        load.start()

    loads[0].wait()
    for pair in range(4):
        flat[2 * pair : 2 * pair + 2, :] = green_v[pair].astype(jnp.float32)
    group = n_e
    for size in (1, 2, 4, 8, 16):
        if size < n_e and n_e % size == 0 and size * per * slab % LANES == 0:
            group = size
            break
    margin = jnp.zeros((8, LANES - slab), jnp.float32)

    @pl.loop(0, n_e // group)
    def _(step):
        window = group * per * slab
        if group == n_e:
            cut = flat[...]
        else:
            cut = flat[:, pl.ds(pl.multiple_of(step * window, LANES), window)]
        for place in range(group * per):
            piece = cut[:, place * slab : (place + 1) * slab]
            lane = place % per * LANES
            chunks[step * group + place // per, :, lane : lane + LANES] = jnp.concatenate(
                [piece, margin], axis=1
            ).astype(jnp.bfloat16)

    beside = (row + n_r - 1) // n_r + (2 * n_r - 2 - row) // n_r
    pl.semaphore_wait(barrier, n_e - 1 + beside)

    def exchange(source, target, send_sem, recv_sem, step):
        other = lax.rem(me + step, n_e)
        return pltpu.make_async_remote_copy(
            src_ref=source.at[other],
            dst_ref=target.at[me],
            send_sem=send_sem.at[step],
            recv_sem=recv_sem.at[me],
            device_id={"energy": other},
            device_id_type=MESH,
        )

    def arrival(source, target, send_sem, recv_sem, step):
        other = lax.rem(me + step, n_e)
        return pltpu.make_async_remote_copy(
            src_ref=source.at[other],
            dst_ref=target.at[other],
            send_sem=send_sem.at[step],
            recv_sem=recv_sem.at[other],
            device_id={"energy": other},
            device_id_type=MESH,
        )

    one = (chunks, land_one, send_one, recv_one)
    two = (chunks_two, land_two, send_two, recv_two)

    @pl.loop(1, n_e)
    def _(step):
        exchange(*one, step).start()

    to_right = pltpu.make_async_remote_copy(
        src_ref=retarded.at[:, :, 2], dst_ref=from_left, send_sem=ret_send.at[0], recv_sem=ret_recv.at[0],
        device_id={"rows": lax.rem(row + 1, n_r)}, device_id_type=MESH,
    )
    to_left = pltpu.make_async_remote_copy(
        src_ref=retarded.at[:, :, 0], dst_ref=from_right, send_sem=ret_send.at[1], recv_sem=ret_recv.at[1],
        device_id={"rows": lax.rem(row + n_r - 1, n_r)}, device_id_type=MESH,
    )

    @pl.when(has_right)
    def _():
        to_right.start()

    @pl.when(has_left)
    def _():
        to_left.start()

    land_one[me] = chunks[me]

    loads[1].wait()
    loads[2].wait()
    count = 4 * total
    energies = (iota((total, total), 0) == order_v[...]).astype(jnp.bfloat16)
    column = iota((total, count), 1)
    slot_of_column = column // 8 * 2 + column % 2
    pick = (iota((total, count), 0) == slot_of_column).astype(jnp.bfloat16)
    hot = dot(energies, pick).astype(jnp.bfloat16)
    shape = (total, count)
    col = iota(shape, 1)
    col_g, col_c = col // 4 % 2, col // 2 % 2
    for part in range(2):
        cosine = dot(tables_v[2 * part, :, :total], hot)
        sine = dot(tables_v[2 * part + 1, :, :total], hot)
        for g in range(2):
            real = jnp.where(col_c == 0, cosine, sine)
            imag = jnp.where(col_c == 0, -sine, cosine)
            base = part * count + g * 2 * total
            forward[base : base + total, :] = jnp.where(col_g == g, real, 0.0).astype(jnp.bfloat16)
            forward[base + total : base + 2 * total, :] = jnp.where(col_g == g, imag, 0.0).astype(jnp.bfloat16)
    half = 2 * total
    line = iota((half, total), 0)
    slot_of_line = line // 4 * 2 + line % 2
    pick_line = (iota((half, total), 1) == slot_of_line).astype(jnp.bfloat16)
    hot_line = lax.dot_general(
        pick_line, energies, (((1,), (1,)), ((), ())), preferred_element_type=jnp.float32
    ).astype(jnp.bfloat16)
    shape = (half, count)
    same_g = iota(shape, 0) // 2 % 2 == iota(shape, 1) // (2 * total)
    from_real = iota(shape, 1) // total % 2 == 0
    scale = 1.0 / total
    for part in range(2):
        cosine = dot(hot_line, tables_v[2 * part]) * scale
        sine = dot(hot_line, tables_v[2 * part + 1]) * scale
        real = jnp.where(from_real, -sine, -cosine)
        imag = jnp.where(from_real, cosine, -sine)
        base = part * count
        backward[base : base + half, :] = jnp.where(same_g, real, 0.0).astype(jnp.bfloat16)
        backward[base + half : base + count, :] = jnp.where(same_g, imag, 0.0).astype(jnp.bfloat16)

    loads[3].wait()
    screen_margin = jnp.zeros((total, LANES - slab), jnp.float32)
    for pair in range(4):
        entries = screen_v[pair].astype(jnp.float32)
        for p in range(per):
            weights[pair * total : (pair + 1) * total, p * LANES : (p + 1) * LANES] = jnp.concatenate(
                [entries[:, p * slab : (p + 1) * slab], screen_margin], axis=1
            )

    lines = 4 * n_e
    line = iota((lines, slab), 0)
    orbital = iota((lines, slab), 1)
    blank = jnp.zeros((LANES - slab, width), jnp.bfloat16)

    def prepare(block, target):
        for slot in range(2):
            real = block[0, slot]
            imag = block[1, slot]
            for side, (upper, lower) in enumerate(((real, imag), (-imag, real))):
                right_side[target, slot, side, 0:slab] = upper
                right_side[target, slot, side, slab:LANES] = blank
                right_side[target, slot, side, LANES : LANES + slab] = lower
                right_side[target, slot, side, LANES + slab :] = blank
            for p in range(per):
                chosen = jnp.where(line % 2 == slot, line // 4 * per + p, -1)
                select = (orbital == chosen).astype(jnp.bfloat16)
                spread[target, slot, 0, p] = dot(select, real)
                spread[target, slot, 1, p] = dot(select, imag)

    loads[4].wait()
    prepare(own_v, 2)

    @pl.loop(1, n_e)
    def _(step):
        arrival(*one, step).wait_recv()

    arrived = land_one[...].reshape(8 * n_e, per * LANES)
    times = dot(forward[...], arrived)
    times = times[:count] + times[count:]
    mixed = []
    for g in range(2):
        base = g * 2 * total
        green_re, green_im = times[base : base + total], times[base + total : base + 2 * total]
        screen_re, screen_im = weights[base : base + total], weights[base + total : base + 2 * total]
        mixed.append(green_re * screen_re - green_im * screen_im)
        mixed.append(green_re * screen_im + green_im * screen_re)
    mixed = jnp.concatenate(mixed, axis=0)
    high = mixed.astype(jnp.bfloat16)
    low = (mixed - high.astype(jnp.float32)).astype(jnp.bfloat16)
    first = dot(backward[...], high)
    sigma = first[:count] + (first[count:] + dot(backward[0:count], low))
    sigma = sigma.astype(jnp.bfloat16)
    for c in range(2):
        for p in range(per):
            lane = (2 * p + c) * LANES
            chunks_two[:, :, lane : lane + LANES] = sigma[
                c * half : (c + 1) * half, p * LANES : (p + 1) * LANES
            ].reshape(n_e, 4, LANES)

    @pl.loop(1, n_e)
    def _(step):
        exchange(*two, step).start()

    land_two[me] = chunks_two[me]

    @pl.when(has_left)
    def _():
        to_right.wait_recv()
        prepare(from_left, 0)

    @pl.when(has_right)
    def _():
        to_left.wait_recv()
        prepare(from_right, 1)

    loads[5].wait()

    @pl.loop(1, n_e)
    def _(step):
        arrival(*two, step).wait_recv()

    for p in range(per):
        rows_two[p] = land_two[:, :, 2 * p * LANES : 2 * (p + 1) * LANES].reshape(lines, 2 * LANES)

    def fold(values):
        values = values.reshape(lines // 8, 8, values.shape[1]).sum(axis=0)
        return values[0:4] + values[4:8]

    def contribution(target):
        real = jnp.zeros((4, width), jnp.float32)
        imag = jnp.zeros((4, width), jnp.float32)
        for p in range(per):
            for slot in range(2):
                inner_re = dot(rows_two[p], right_side[target, slot, 0])
                inner_im = dot(rows_two[p], right_side[target, slot, 1])
                outer_re = spread[target, slot, 0, p]
                outer_im = spread[target, slot, 1, p]
                real = real + fold(outer_re * inner_re - outer_im * inner_im)
                imag = imag + fold(outer_re * inner_im + outer_im * inner_re)
        return jnp.concatenate([real, imag], axis=0)

    back_left = pltpu.make_async_remote_copy(
        src_ref=halo_out.at[0], dst_ref=halo_in.at[1], send_sem=halo_send.at[0], recv_sem=halo_recv.at[1],
        device_id={"rows": lax.rem(row + n_r - 1, n_r)}, device_id_type=MESH,
    )
    back_right = pltpu.make_async_remote_copy(
        src_ref=halo_out.at[1], dst_ref=halo_in.at[0], send_sem=halo_send.at[1], recv_sem=halo_recv.at[0],
        device_id={"rows": lax.rem(row + 1, n_r)}, device_id_type=MESH,
    )

    @pl.when(row == 0)
    def _():
        halo_in[0] = jnp.zeros(halo_in.shape[1:], jnp.float32)

    @pl.when(row == n_r - 1)
    def _():
        halo_in[1] = jnp.zeros(halo_in.shape[1:], jnp.float32)

    @pl.when(has_left)
    def _():
        halo_out[0] = contribution(0)
        back_left.start()

    @pl.when(has_right)
    def _():
        halo_out[1] = contribution(1)
        back_right.start()

    density = contribution(2)
    direct = [jnp.zeros((4, LANES), jnp.float32), jnp.zeros((4, LANES), jnp.float32)]
    shape = (lines, LANES)
    for p in range(per):
        on_diagonal = iota(shape, 1) == iota(shape, 0) // 4 * per + p
        for c in range(2):
            entries = rows_two[p, :, c * LANES : (c + 1) * LANES].astype(jnp.float32)
            direct[c] = direct[c] + fold(jnp.where(on_diagonal, entries, 0.0))
    shape = (LANES, width)
    place = iota(shape, 1) == iota(shape, 0) + start_v[0]
    density = density + dot(
        jnp.concatenate(direct, axis=0).astype(jnp.bfloat16), place.astype(jnp.bfloat16)
    )

    @pl.when(has_left)
    def _():
        back_right.wait_recv()

    @pl.when(has_right)
    def _():
        back_left.wait_recv()

    density = density + halo_in[0] + halo_in[1]
    for c in range(2):
        for g in range(2):
            out[g, c] = density[4 * c + 2 * g : 4 * c + 2 * g + 2]

    @pl.loop(1, n_e)
    def _(step):
        exchange(*one, step).wait_send()
        exchange(*two, step).wait_send()

    @pl.when(has_right)
    def _():
        to_right.wait_send()
        back_right.wait_send()

    @pl.when(has_left)
    def _():
        to_left.wait_send()
        back_left.wait_send()


def shards(green_window, screened, retarded, energy_order, window_start):
    n_e = lax.axis_size("energy")
    entries = green_window.shape[4]
    columns = screened.shape[4]
    total = screened.shape[2]
    slab, width = retarded.shape[4], retarded.shape[5]
    per = slab // n_e
    half = jnp.bfloat16
    full = jnp.float32
    lines = 4 * n_e
    scratch = [
        pltpu.VMEM((4, 2, entries), half),
        pltpu.VMEM((4, total, columns), half),
        pltpu.VMEM((2, 2, slab, width), half),
        pltpu.VMEM((1, total), jnp.int32),
        pltpu.SMEM((1,), jnp.int32),
        pltpu.VMEM((4, total, 4 * total), half),
        pltpu.VMEM((8, entries), full),
        pltpu.VMEM((n_e, 8, per * LANES), half),
        pltpu.VMEM((n_e, 8, per * LANES), half),
        pltpu.VMEM((4 * total, per * LANES), full),
        pltpu.VMEM((8 * total, 4 * total), half),
        pltpu.VMEM((8 * total, 4 * total), half),
        pltpu.VMEM((n_e, 4, 2 * per * LANES), half),
        pltpu.VMEM((n_e, 4, 2 * per * LANES), half),
        pltpu.VMEM((per, lines, 2 * LANES), half),
        pltpu.VMEM((2, 2, slab, width), half),
        pltpu.VMEM((2, 2, slab, width), half),
        pltpu.VMEM((3, 2, 2, 2 * LANES, width), half),
        pltpu.VMEM((3, 2, 2, per, lines, width), full),
        pltpu.VMEM((2, 8, width), full),
        pltpu.VMEM((2, 8, width), full),
        pltpu.SemaphoreType.DMA((6,)),
        pltpu.SemaphoreType.DMA((n_e,)),
        pltpu.SemaphoreType.DMA((n_e,)),
        pltpu.SemaphoreType.DMA((n_e,)),
        pltpu.SemaphoreType.DMA((n_e,)),
        pltpu.SemaphoreType.DMA((2,)),
        pltpu.SemaphoreType.DMA((2,)),
        pltpu.SemaphoreType.DMA((2,)),
        pltpu.SemaphoreType.DMA((2,)),
    ]
    anywhere = pl.BlockSpec(memory_space=pl.ANY)
    density = pl.pallas_call(
        kernel,
        out_shape=jax.ShapeDtypeStruct((2, 2, 2, width), full),
        in_specs=[anywhere] * 6,
        out_specs=pl.BlockSpec(memory_space=pltpu.VMEM),
        scratch_shapes=scratch,
        compiler_params=pltpu.CompilerParams(
            collective_id=0, has_side_effects=True, vmem_limit_bytes=48 * 2**20
        ),
    )(
        green_window.reshape(4, 2, entries),
        screened.reshape(4, total, columns),
        retarded[:, :, 0],
        energy_order.reshape(1, total),
        window_start,
        jnp.asarray(phase_tables(total)),
    )
    return density[:, :, :, None, :]


def solution(mesh):
    in_specs = (
        P(None, None, "energy", "rows", None),
        P(None, None, None, "rows", "energy"),
        P(None, "energy", "rows", None, None, None),
        P(),
        P("rows"),
    )
    out_specs = P(None, None, "energy", "rows", None)
    return jax.shard_map(shards, mesh=mesh, in_specs=in_specs, out_specs=out_specs, check_vma=False)
```

```python
import functools
import math

import jax
import jax.numpy as jnp
import numpy as np
from jax import lax
from jax.experimental import pallas as pl
from jax.experimental.pallas import tpu as pltpu
from jax.sharding import PartitionSpec as P

MESH = pl.DeviceIdType.MESH
LANES = 128


def phase_tables(total):
    turns = np.outer(np.arange(total), np.arange(total)) % total
    angle = 2.0 * math.pi / total * turns
    parts = []
    for exact in (np.cos(angle), np.sin(angle)):
        high = exact.astype(jnp.bfloat16)
        low = (exact - high.astype(np.float64)).astype(jnp.bfloat16)
        parts.append((high, low))
    stacked = np.stack([parts[0][0], parts[1][0], parts[0][1], parts[1][1]])
    return np.tile(stacked, (1, 1, 4))


def dot(left, right):
    return jnp.dot(left, right, preferred_element_type=jnp.float32)


def iota(shape, axis):
    return lax.broadcasted_iota(jnp.int32, shape, axis)


def kernel(
    green, screened, retarded, order, start, tables, out,
    green_v, screen_v, own_v, order_v, start_v, tables_v,
    flat, chunks, land_one, weights, forward, backward,
    chunks_two, land_two, rows_two, land_far, rows_far, far_v, from_left, from_right, right_side, spread, halo_out, halo_in,
    local_sem, send_one, recv_one, send_two, recv_two, send_far, recv_far, ret_send, ret_recv, halo_send, halo_recv,
):
    n_e = lax.axis_size("energy")
    n_r = lax.axis_size("rows")
    me = lax.axis_index("energy")
    row = lax.axis_index("rows")
    slab, width = own_v.shape[2], own_v.shape[3]
    total = order_v.shape[1]
    per = slab // n_e
    middle = n_r // 2
    far_row = 2 * middle - 1 - row
    far_side = middle - row
    is_far = jnp.logical_or(row == middle - 1, row == middle)
    has_left = jnp.logical_and(row > 0, row != middle)
    has_right = jnp.logical_and(row < n_r - 1, row != middle - 1)

    barrier = pltpu.get_barrier_semaphore()

    @pl.loop(1, n_e)
    def _(step):
        pl.semaphore_signal(
            barrier, inc=1, device_id={"energy": lax.rem(me + step, n_e)}, device_id_type=MESH
        )

    @pl.when(row > 0)
    def _():
        pl.semaphore_signal(barrier, inc=1, device_id={"rows": row - 1}, device_id_type=MESH)

    @pl.when(row < n_r - 1)
    def _():
        pl.semaphore_signal(barrier, inc=1, device_id={"rows": row + 1}, device_id_type=MESH)

    loads = [
        pltpu.make_async_copy(green, green_v, local_sem.at[0]),
        pltpu.make_async_copy(order, order_v, local_sem.at[1]),
        pltpu.make_async_copy(tables, tables_v, local_sem.at[2]),
        pltpu.make_async_copy(screened, screen_v, local_sem.at[3]),
        pltpu.make_async_copy(retarded.at[:, :, 1], own_v, local_sem.at[4]),
        pltpu.make_async_copy(start, start_v, local_sem.at[5]),
    ]
    for load in loads:
        load.start()
    far_load = pltpu.make_async_copy(retarded.at[:, :, 2 * far_side], far_v, local_sem.at[6])

    @pl.when(is_far)
    def _():
        far_load.start()

    loads[0].wait()
    for pair in range(4):
        flat[2 * pair : 2 * pair + 2, :] = green_v[pair].astype(jnp.float32)
    group = n_e
    for size in (1, 2, 4, 8, 16):
        if size < n_e and n_e % size == 0 and size * per * slab % LANES == 0:
            group = size
            break
    margin = jnp.zeros((8, LANES - slab), jnp.float32)

    @pl.loop(0, n_e // group)
    def _(step):
        window = group * per * slab
        if group == n_e:
            cut = flat[...]
        else:
            cut = flat[:, pl.ds(pl.multiple_of(step * window, LANES), window)]
        for place in range(group * per):
            piece = cut[:, place * slab : (place + 1) * slab]
            lane = place % per * LANES
            chunks[step * group + place // per, :, lane : lane + LANES] = jnp.concatenate(
                [piece, margin], axis=1
            ).astype(jnp.bfloat16)

    beside = (row + n_r - 1) // n_r + (2 * n_r - 2 - row) // n_r
    pl.semaphore_wait(barrier, n_e - 1 + beside)

    def exchange(source, target, send_sem, recv_sem, step):
        other = lax.rem(me + step, n_e)
        return pltpu.make_async_remote_copy(
            src_ref=source.at[other],
            dst_ref=target.at[me],
            send_sem=send_sem.at[step],
            recv_sem=recv_sem.at[me],
            device_id={"energy": other},
            device_id_type=MESH,
        )

    def arrival(source, target, send_sem, recv_sem, step):
        other = lax.rem(me + step, n_e)
        return pltpu.make_async_remote_copy(
            src_ref=source.at[other],
            dst_ref=target.at[other],
            send_sem=send_sem.at[step],
            recv_sem=recv_sem.at[other],
            device_id={"energy": other},
            device_id_type=MESH,
        )

    def cross(step, device):
        return pltpu.make_async_remote_copy(
            src_ref=chunks_two.at[step],
            dst_ref=land_far.at[device],
            send_sem=send_far.at[step],
            recv_sem=recv_far.at[device],
            device_id={"energy": step, "rows": far_row},
            device_id_type=MESH,
        )

    one = (chunks, land_one, send_one, recv_one)
    two = (chunks_two, land_two, send_two, recv_two)

    @pl.loop(1, n_e)
    def _(step):
        exchange(*one, step).start()

    to_right = pltpu.make_async_remote_copy(
        src_ref=retarded.at[:, :, 2], dst_ref=from_left, send_sem=ret_send.at[0], recv_sem=ret_recv.at[0],
        device_id={"rows": lax.rem(row + 1, n_r)}, device_id_type=MESH,
    )
    to_left = pltpu.make_async_remote_copy(
        src_ref=retarded.at[:, :, 0], dst_ref=from_right, send_sem=ret_send.at[1], recv_sem=ret_recv.at[1],
        device_id={"rows": lax.rem(row + n_r - 1, n_r)}, device_id_type=MESH,
    )

    @pl.when(has_right)
    def _():
        to_right.start()

    @pl.when(has_left)
    def _():
        to_left.start()

    land_one[me] = chunks[me]

    loads[1].wait()
    loads[2].wait()
    count = 4 * total
    energies = (iota((total, total), 0) == order_v[...]).astype(jnp.bfloat16)
    column = iota((total, count), 1)
    slot_of_column = column // 8 * 2 + column % 2
    pick = (iota((total, count), 0) == slot_of_column).astype(jnp.bfloat16)
    hot = dot(energies, pick).astype(jnp.bfloat16)
    shape = (total, count)
    col = iota(shape, 1)
    col_g, col_c = col // 4 % 2, col // 2 % 2
    for part in range(2):
        cosine = dot(tables_v[2 * part, :, :total], hot)
        sine = dot(tables_v[2 * part + 1, :, :total], hot)
        for g in range(2):
            real = jnp.where(col_c == 0, cosine, sine)
            imag = jnp.where(col_c == 0, -sine, cosine)
            base = part * count + g * 2 * total
            forward[base : base + total, :] = jnp.where(col_g == g, real, 0.0).astype(jnp.bfloat16)
            forward[base + total : base + 2 * total, :] = jnp.where(col_g == g, imag, 0.0).astype(jnp.bfloat16)
    half = 2 * total
    line = iota((half, total), 0)
    slot_of_line = line // 4 * 2 + line % 2
    pick_line = (iota((half, total), 1) == slot_of_line).astype(jnp.bfloat16)
    hot_line = lax.dot_general(
        pick_line, energies, (((1,), (1,)), ((), ())), preferred_element_type=jnp.float32
    ).astype(jnp.bfloat16)
    shape = (half, count)
    same_g = iota(shape, 0) // 2 % 2 == iota(shape, 1) // (2 * total)
    from_real = iota(shape, 1) // total % 2 == 0
    scale = 1.0 / total
    for part in range(2):
        cosine = dot(hot_line, tables_v[2 * part]) * scale
        sine = dot(hot_line, tables_v[2 * part + 1]) * scale
        real = jnp.where(from_real, -sine, -cosine)
        imag = jnp.where(from_real, cosine, -sine)
        base = part * count
        backward[base : base + half, :] = jnp.where(same_g, real, 0.0).astype(jnp.bfloat16)
        backward[base + half : base + count, :] = jnp.where(same_g, imag, 0.0).astype(jnp.bfloat16)

    loads[3].wait()
    screen_margin = jnp.zeros((total, LANES - slab), jnp.float32)
    for pair in range(4):
        entries = screen_v[pair].astype(jnp.float32)
        for p in range(per):
            weights[pair * total : (pair + 1) * total, p * LANES : (p + 1) * LANES] = jnp.concatenate(
                [entries[:, p * slab : (p + 1) * slab], screen_margin], axis=1
            )

    lines = 4 * n_e
    line = iota((lines, slab), 0)
    orbital = iota((lines, slab), 1)
    blank = jnp.zeros((LANES - slab, width), jnp.bfloat16)

    def prepare(block, target):
        for slot in range(2):
            real = block[0, slot]
            imag = block[1, slot]
            for side, (upper, lower) in enumerate(((real, imag), (-imag, real))):
                right_side[target, slot, side, 0:slab] = upper
                right_side[target, slot, side, slab:LANES] = blank
                right_side[target, slot, side, LANES : LANES + slab] = lower
                right_side[target, slot, side, LANES + slab :] = blank
            for p in range(per):
                chosen = jnp.where(line % 2 == slot, line // 4 * per + p, -1)
                select = (orbital == chosen).astype(jnp.bfloat16)
                spread[target, slot, 0, p] = dot(select, real)
                spread[target, slot, 1, p] = dot(select, imag)

    loads[4].wait()
    prepare(own_v, 2)

    @pl.when(is_far)
    def _():
        far_load.wait()
        prepare(far_v, far_side)

    @pl.loop(1, n_e)
    def _(step):
        arrival(*one, step).wait_recv()

    arrived = land_one[...].reshape(8 * n_e, per * LANES)
    times = dot(forward[...], arrived)
    times = times[:count] + times[count:]
    mixed = []
    for g in range(2):
        base = g * 2 * total
        green_re, green_im = times[base : base + total], times[base + total : base + 2 * total]
        screen_re, screen_im = weights[base : base + total], weights[base + total : base + 2 * total]
        mixed.append(green_re * screen_re - green_im * screen_im)
        mixed.append(green_re * screen_im + green_im * screen_re)
    mixed = jnp.concatenate(mixed, axis=0)
    high = mixed.astype(jnp.bfloat16)
    low = (mixed - high.astype(jnp.float32)).astype(jnp.bfloat16)
    first = dot(backward[...], high)
    sigma = first[:count] + (first[count:] + dot(backward[0:count], low))
    sigma = sigma.astype(jnp.bfloat16)
    for c in range(2):
        for p in range(per):
            lane = (2 * p + c) * LANES
            chunks_two[:, :, lane : lane + LANES] = sigma[
                c * half : (c + 1) * half, p * LANES : (p + 1) * LANES
            ].reshape(n_e, 4, LANES)

    @pl.loop(1, n_e)
    def _(step):
        exchange(*two, step).start()

    @pl.when(is_far)
    def _():
        @pl.loop(0, n_e)
        def _(step):
            cross(lax.rem(me + step, n_e), me).start()

    land_two[me] = chunks_two[me]

    @pl.when(has_left)
    def _():
        to_right.wait_recv()
        prepare(from_left, 0)

    @pl.when(has_right)
    def _():
        to_left.wait_recv()
        prepare(from_right, 1)

    loads[5].wait()

    @pl.loop(1, n_e)
    def _(step):
        arrival(*two, step).wait_recv()

    def regroup(landed, grouped):
        for p in range(per):
            grouped[p] = landed[:, :, 2 * p * LANES : 2 * (p + 1) * LANES].reshape(lines, 2 * LANES)

    regroup(land_two, rows_two)

    def fold(values):
        values = values.reshape(lines // 8, 8, values.shape[1]).sum(axis=0)
        return values[0:4] + values[4:8]

    def contribution(target, grouped):
        real = jnp.zeros((4, width), jnp.float32)
        imag = jnp.zeros((4, width), jnp.float32)
        for p in range(per):
            for slot in range(2):
                inner_re = dot(grouped[p], right_side[target, slot, 0])
                inner_im = dot(grouped[p], right_side[target, slot, 1])
                outer_re = spread[target, slot, 0, p]
                outer_im = spread[target, slot, 1, p]
                real = real + fold(outer_re * inner_re - outer_im * inner_im)
                imag = imag + fold(outer_re * inner_im + outer_im * inner_re)
        return jnp.concatenate([real, imag], axis=0)

    back_left = pltpu.make_async_remote_copy(
        src_ref=halo_out.at[0], dst_ref=halo_in.at[1], send_sem=halo_send.at[0], recv_sem=halo_recv.at[1],
        device_id={"rows": lax.rem(row + n_r - 1, n_r)}, device_id_type=MESH,
    )
    back_right = pltpu.make_async_remote_copy(
        src_ref=halo_out.at[1], dst_ref=halo_in.at[0], send_sem=halo_send.at[1], recv_sem=halo_recv.at[0],
        device_id={"rows": lax.rem(row + 1, n_r)}, device_id_type=MESH,
    )

    @pl.when(jnp.logical_not(has_left))
    def _():
        halo_in[0] = jnp.zeros(halo_in.shape[1:], jnp.float32)

    @pl.when(jnp.logical_not(has_right))
    def _():
        halo_in[1] = jnp.zeros(halo_in.shape[1:], jnp.float32)

    @pl.when(has_left)
    def _():
        halo_out[0] = contribution(0, rows_two)
        back_left.start()

    @pl.when(has_right)
    def _():
        halo_out[1] = contribution(1, rows_two)
        back_right.start()

    density = contribution(2, rows_two)
    direct = [jnp.zeros((4, LANES), jnp.float32), jnp.zeros((4, LANES), jnp.float32)]
    shape = (lines, LANES)
    for p in range(per):
        on_diagonal = iota(shape, 1) == iota(shape, 0) // 4 * per + p
        for c in range(2):
            entries = rows_two[p, :, c * LANES : (c + 1) * LANES].astype(jnp.float32)
            direct[c] = direct[c] + fold(jnp.where(on_diagonal, entries, 0.0))
    shape = (LANES, width)
    place = iota(shape, 1) == iota(shape, 0) + start_v[...]
    density = density + dot(
        jnp.concatenate(direct, axis=0).astype(jnp.bfloat16), place.astype(jnp.bfloat16)
    )

    @pl.when(is_far)
    def _():
        @pl.loop(0, n_e)
        def _(step):
            cross(step, step).wait_recv()

        regroup(land_far, rows_far)
        halo_in[far_side] = contribution(far_side, rows_far)

    @pl.when(has_left)
    def _():
        back_right.wait_recv()

    @pl.when(has_right)
    def _():
        back_left.wait_recv()

    density = density + halo_in[0] + halo_in[1]
    for c in range(2):
        for g in range(2):
            out[g, c] = density[4 * c + 2 * g : 4 * c + 2 * g + 2]

    @pl.loop(1, n_e)
    def _(step):
        exchange(*one, step).wait_send()
        exchange(*two, step).wait_send()

    @pl.when(is_far)
    def _():
        @pl.loop(0, n_e)
        def _(step):
            cross(step, me).wait_send()

    @pl.when(has_right)
    def _():
        to_right.wait_send()
        back_right.wait_send()

    @pl.when(has_left)
    def _():
        to_left.wait_send()
        back_left.wait_send()


def shards(green_window, screened, retarded, energy_order, window_start):
    n_e = lax.axis_size("energy")
    entries = green_window.shape[4]
    columns = screened.shape[4]
    total = screened.shape[2]
    slab, width = retarded.shape[4], retarded.shape[5]
    per = slab // n_e
    half = jnp.bfloat16
    full = jnp.float32
    lines = 4 * n_e
    scratch = [
        pltpu.VMEM((4, 2, entries), half),
        pltpu.VMEM((4, total, columns), half),
        pltpu.VMEM((2, 2, slab, width), half),
        pltpu.VMEM((1, total), jnp.int32),
        pltpu.VMEM((1, 1), jnp.int32),
        pltpu.VMEM((4, total, 4 * total), half),
        pltpu.VMEM((8, entries), full),
        pltpu.VMEM((n_e, 8, per * LANES), half),
        pltpu.VMEM((n_e, 8, per * LANES), half),
        pltpu.VMEM((4 * total, per * LANES), full),
        pltpu.VMEM((8 * total, 4 * total), half),
        pltpu.VMEM((8 * total, 4 * total), half),
        pltpu.VMEM((n_e, 4, 2 * per * LANES), half),
        pltpu.VMEM((n_e, 4, 2 * per * LANES), half),
        pltpu.VMEM((per, lines, 2 * LANES), half),
        pltpu.VMEM((n_e, 4, 2 * per * LANES), half),
        pltpu.VMEM((per, lines, 2 * LANES), half),
        pltpu.VMEM((2, 2, slab, width), half),
        pltpu.VMEM((2, 2, slab, width), half),
        pltpu.VMEM((2, 2, slab, width), half),
        pltpu.VMEM((3, 2, 2, 2 * LANES, width), half),
        pltpu.VMEM((3, 2, 2, per, lines, width), full),
        pltpu.VMEM((2, 8, width), full),
        pltpu.VMEM((2, 8, width), full),
        pltpu.SemaphoreType.DMA((7,)),
        pltpu.SemaphoreType.DMA((n_e,)),
        pltpu.SemaphoreType.DMA((n_e,)),
        pltpu.SemaphoreType.DMA((n_e,)),
        pltpu.SemaphoreType.DMA((n_e,)),
        pltpu.SemaphoreType.DMA((n_e,)),
        pltpu.SemaphoreType.DMA((n_e,)),
        pltpu.SemaphoreType.DMA((2,)),
        pltpu.SemaphoreType.DMA((2,)),
        pltpu.SemaphoreType.DMA((2,)),
        pltpu.SemaphoreType.DMA((2,)),
    ]
    anywhere = pl.BlockSpec(memory_space=pltpu.HBM)
    density = pl.pallas_call(
        kernel,
        out_shape=jax.ShapeDtypeStruct((2, 2, 2, width), full),
        in_specs=[anywhere] * 6,
        out_specs=pl.BlockSpec(memory_space=pltpu.VMEM),
        scratch_shapes=scratch,
        compiler_params=pltpu.CompilerParams(
            collective_id=0, has_side_effects=True, vmem_limit_bytes=67043328
        ),
    )(
        green_window.reshape(4, 2, entries),
        screened.reshape(4, total, columns),
        retarded[:, :, 0],
        energy_order.reshape(1, total),
        window_start.reshape(1, 1),
        jnp.asarray(phase_tables(total)),
    )
    return density[:, :, :, None, :]


def solution(mesh):
    in_specs = (
        P(None, None, "energy", "rows", None),
        P(None, None, None, "rows", "energy"),
        P(None, "energy", "rows", None, None, None),
        P(),
        P("rows"),
    )
    out_specs = P(None, None, "energy", "rows", None)
    return jax.shard_map(shards, mesh=mesh, in_specs=in_specs, out_specs=out_specs, check_vma=False)
```

```python
import functools
import math

import jax
import jax.numpy as jnp
import numpy as np
from jax import lax
from jax.experimental import pallas as pl
from jax.experimental.pallas import tpu as pltpu
from jax.sharding import PartitionSpec as P

MESH = pl.DeviceIdType.MESH
PLANES = 8
LANES = 128


def phase_tables(total):
    turns = np.outer(np.arange(total), np.arange(total)) % total
    angle = 2.0 * math.pi / total * turns
    parts = []
    for exact in (np.cos(angle), np.sin(angle)):
        high = exact.astype(jnp.bfloat16)
        low = (exact - high.astype(np.float64)).astype(jnp.bfloat16)
        parts.append((high, low))
    stacked = np.stack([parts[0][0], parts[1][0], parts[0][1], parts[1][1]])
    return np.tile(stacked, (1, 1, 4))


def dot(left, right):
    return jnp.dot(left, right, preferred_element_type=jnp.float32)


def iota(shape, axis):
    return lax.broadcasted_iota(jnp.int32, shape, axis)


def kernel(
    green, screened, retarded, order, tables, start, out,
    green_v, screen_v, own_v, order_v, tables_v,
    flat, chunks, land_one, weights, forward, backward,
    chunks_two, land_two, rows_two, land_far, rows_far, far_v, from_left, from_right, right_side, spread, halo_out, halo_in,
    local_sem, send_one, recv_one, send_two, recv_two, send_far, recv_far, ret_send, ret_recv, halo_send, halo_recv,
):
    n_e = lax.axis_size("energy")
    n_r = lax.axis_size("rows")
    me = lax.axis_index("energy")
    row = lax.axis_index("rows")
    slab, width = own_v.shape[2], own_v.shape[3]
    total = order_v.shape[1]
    per = slab // n_e
    middle = n_r // 2
    far_row = 2 * middle - 1 - row
    far_side = middle - row
    is_far = jnp.logical_or(row == middle - 1, row == middle)
    has_left = jnp.logical_and(row > 0, row != middle)
    has_right = jnp.logical_and(row < n_r - 1, row != middle - 1)

    barrier = pltpu.get_barrier_semaphore()

    @pl.loop(0, n_e)
    def _(step):
        other = lax.rem(me + 1 + step, n_e)

        @pl.when(other != me)
        def _():
            pl.semaphore_signal(barrier, inc=1, device_id={"energy": other}, device_id_type=MESH)

    @pl.when(row > 0)
    def _():
        pl.semaphore_signal(barrier, inc=1, device_id={"rows": row - 1}, device_id_type=MESH)

    @pl.when(row < n_r - 1)
    def _():
        pl.semaphore_signal(barrier, inc=1, device_id={"rows": row + 1}, device_id_type=MESH)

    loads = [
        pltpu.make_async_copy(green, green_v, local_sem.at[0]),
        pltpu.make_async_copy(order, order_v, local_sem.at[1]),
        pltpu.make_async_copy(tables, tables_v, local_sem.at[2]),
        pltpu.make_async_copy(screened, screen_v, local_sem.at[3]),
        pltpu.make_async_copy(retarded.at[:, :, 1], own_v, local_sem.at[4]),
    ]
    for load in loads:
        load.start()
    far_load = pltpu.make_async_copy(retarded.at[:, :, 2 * far_side], far_v, local_sem.at[6])

    @pl.when(is_far)
    def _():
        far_load.start()

    loads[0].wait()
    for pair in range(4):
        flat[2 * pair : 2 * pair + 2, :] = green_v[pair].astype(jnp.float32)
    group = n_e
    for size in (1, 2, 4, 8, 16):
        if size < n_e and n_e % size == 0 and size * per * slab % LANES == 0:
            group = size
            break
    margin = jnp.zeros((8, LANES - slab), jnp.float32)

    @pl.loop(0, n_e // group)
    def _(step):
        window = group * per * slab
        if group == n_e:
            cut = flat[...]
        else:
            cut = flat[:, pl.ds(pl.multiple_of(step * window, LANES), window)]
        for place in range(group * per):
            piece = cut[:, place * slab : (place + 1) * slab]
            lane = place % per * LANES
            chunks[step * group + place // per, :, lane : lane + LANES] = jnp.concatenate(
                [piece, margin], axis=1
            ).astype(jnp.bfloat16)

    beside = (row + n_r - 1) // n_r + (2 * n_r - 2 - row) // n_r
    pl.semaphore_wait(barrier, n_e - 1 + beside)

    def exchange(source, target, send_sem, recv_sem, other):
        return pltpu.make_async_remote_copy(
            src_ref=source.at[other],
            dst_ref=target.at[me],
            send_sem=send_sem.at[other],
            recv_sem=recv_sem.at[me],
            device_id={"energy": other},
            device_id_type=MESH,
        )

    def arrival(source, target, send_sem, recv_sem, other):
        return pltpu.make_async_remote_copy(
            src_ref=source.at[other],
            dst_ref=target.at[other],
            send_sem=send_sem.at[other],
            recv_sem=recv_sem.at[other],
            device_id={"energy": other},
            device_id_type=MESH,
        )

    def cross(step, device):
        return pltpu.make_async_remote_copy(
            src_ref=chunks_two.at[step],
            dst_ref=land_far.at[device],
            send_sem=send_far.at[step],
            recv_sem=recv_far.at[device],
            device_id={"energy": step, "rows": far_row},
            device_id_type=MESH,
        )

    one = (chunks, land_one, send_one, recv_one)
    two = (chunks_two, land_two, send_two, recv_two)

    @pl.loop(0, n_e)
    def _(step):
        other = lax.rem(me + 1 + step, n_e)

        @pl.when(other != me)
        def _():
            exchange(*one, other).start()

    to_right = pltpu.make_async_remote_copy(
        src_ref=retarded.at[:, :, 2], dst_ref=from_left, send_sem=ret_send.at[0], recv_sem=ret_recv.at[0],
        device_id={"rows": lax.rem(row + 1, n_r)}, device_id_type=MESH,
    )
    to_left = pltpu.make_async_remote_copy(
        src_ref=retarded.at[:, :, 0], dst_ref=from_right, send_sem=ret_send.at[1], recv_sem=ret_recv.at[1],
        device_id={"rows": lax.rem(row + n_r - 1, n_r)}, device_id_type=MESH,
    )

    @pl.when(has_right)
    def _():
        to_right.start()

    @pl.when(has_left)
    def _():
        to_left.start()

    land_one[me] = chunks[me]

    loads[1].wait()
    loads[2].wait()
    count = 4 * total
    energies = (iota((total, total), 0) == order_v[...]).astype(jnp.bfloat16)
    column = iota((total, count), 1)
    slot_of_column = column // 8 * 2 + column % 2
    pick = (iota((total, count), 0) == slot_of_column).astype(jnp.bfloat16)
    hot = dot(energies, pick).astype(jnp.bfloat16)
    shape = (total, count)
    col = iota(shape, 1)
    col_g, col_c = col // 4 % 2, col // 2 % 2
    for part in range(2):
        cosine = dot(tables_v[2 * part, :, :total], hot)
        sine = dot(tables_v[2 * part + 1, :, :total], hot)
        for g in range(2):
            real = jnp.where(col_c == 0, cosine, sine)
            imag = jnp.where(col_c == 0, -sine, cosine)
            base = part * count + g * 2 * total
            forward[base : base + total, :] = jnp.where(col_g == g, real, 0.0).astype(jnp.bfloat16)
            forward[base + total : base + 2 * total, :] = jnp.where(col_g == g, imag, 0.0).astype(jnp.bfloat16)
    half = 2 * total
    line = iota((half, total), 0)
    slot_of_line = line // 4 * 2 + line % 2
    pick_line = (iota((half, total), 1) == slot_of_line).astype(jnp.bfloat16)
    hot_line = lax.dot_general(
        pick_line, energies, (((1,), (1,)), ((), ())), preferred_element_type=jnp.float32
    ).astype(jnp.bfloat16)
    shape = (half, count)
    same_g = iota(shape, 0) // 2 % 2 == iota(shape, 1) // (2 * total)
    from_real = iota(shape, 1) // total % 2 == 0
    scale = 1.0 / total
    for part in range(2):
        cosine = dot(hot_line, tables_v[2 * part]) * scale
        sine = dot(hot_line, tables_v[2 * part + 1]) * scale
        real = jnp.where(from_real, -sine, -cosine)
        imag = jnp.where(from_real, cosine, -sine)
        base = part * count
        backward[base : base + half, :] = jnp.where(same_g, real, 0.0).astype(jnp.bfloat16)
        backward[base + half : base + count, :] = jnp.where(same_g, imag, 0.0).astype(jnp.bfloat16)

    loads[3].wait()
    screen_margin = jnp.zeros((total, LANES - slab), jnp.float32)
    for pair in range(4):
        entries = screen_v[pair].astype(jnp.float32)
        for p in range(per):
            weights[pair * total : (pair + 1) * total, p * LANES : (p + 1) * LANES] = jnp.concatenate(
                [entries[:, p * slab : (p + 1) * slab], screen_margin], axis=1
            )

    lines = 4 * n_e
    line = iota((lines, slab), 0)
    orbital = iota((lines, slab), 1)
    blank = jnp.zeros((LANES - slab, width), jnp.bfloat16)

    def prepare(block, target):
        for slot in range(2):
            real = block[0, slot]
            imag = block[1, slot]
            for side, (upper, lower) in enumerate(((real, imag), (-imag, real))):
                right_side[target, slot, side, 0:slab] = upper
                right_side[target, slot, side, slab:LANES] = blank
                right_side[target, slot, side, LANES : LANES + slab] = lower
                right_side[target, slot, side, LANES + slab :] = blank
            for p in range(per):
                chosen = jnp.where(line % 2 == slot, line // 4 * per + p, -1)
                select = (orbital == chosen).astype(jnp.bfloat16)
                for part, values in enumerate((real, imag)):
                    rows = dot(select, values)
                    spread[target, part, p] = rows if slot == 0 else spread[target, part, p] + rows

    loads[4].wait()
    prepare(own_v, 2)

    @pl.when(is_far)
    def _():
        far_load.wait()
        prepare(far_v, far_side)

    @pl.loop(1, n_e)
    def _(step):
        arrival(*one, lax.rem(me + step, n_e)).wait_recv()

    arrived = land_one[...].reshape(8 * n_e, per * LANES)
    times = dot(forward[...], arrived)
    times = times[:count] + times[count:]
    mixed = []
    for g in range(2):
        base = g * 2 * total
        green_re, green_im = times[base : base + total], times[base + total : base + 2 * total]
        screen_re, screen_im = weights[base : base + total], weights[base + total : base + 2 * total]
        mixed.append(green_re * screen_re - green_im * screen_im)
        mixed.append(green_re * screen_im + green_im * screen_re)
    mixed = jnp.concatenate(mixed, axis=0)
    high = mixed.astype(jnp.bfloat16)
    low = (mixed - high.astype(jnp.float32)).astype(jnp.bfloat16)
    first = dot(backward[...], high)
    sigma = first[:count] + (first[count:] + dot(backward[0:count], low))
    sigma = sigma.astype(jnp.bfloat16)
    for c in range(2):
        for p in range(per):
            lane = (2 * p + c) * LANES
            chunks_two[:, :, lane : lane + LANES] = sigma[
                c * half : (c + 1) * half, p * LANES : (p + 1) * LANES
            ].reshape(n_e, 4, LANES)

    plane = max(1, n_e // PLANES)

    @pl.loop(0, n_e)
    def _(step):
        other = step // plane * plane + lax.rem(me + step, plane)

        @pl.when(other != me)
        def _():
            exchange(*two, other).start()

    @pl.when(is_far)
    def _():
        @pl.loop(0, n_e)
        def _(step):
            cross(step // plane * plane + lax.rem(me + step, plane), me).start()

    land_two[me] = chunks_two[me]

    @pl.when(has_left)
    def _():
        to_right.wait_recv()
        prepare(from_left, 0)

    @pl.when(has_right)
    def _():
        to_left.wait_recv()
        prepare(from_right, 1)

    @pl.loop(1, n_e)
    def _(step):
        exchange(*one, lax.rem(me + step, n_e)).wait_send()

    @pl.loop(1, n_e)
    def _(step):
        arrival(*two, lax.rem(me + step, n_e)).wait_recv()

    def regroup(landed, grouped):
        for p in range(per):
            grouped[p] = landed[:, :, 2 * p * LANES : 2 * (p + 1) * LANES].reshape(lines, 2 * LANES)

    regroup(land_two, rows_two)

    def fold(values):
        values = values.reshape(lines // 8, 8, values.shape[1]).sum(axis=0)
        return values[0:4] + values[4:8]

    first_slot = iota((lines, width), 0) % 2 == 0

    def contribution(target, grouped):
        real = jnp.zeros((4, width), jnp.float32)
        imag = jnp.zeros((4, width), jnp.float32)
        for p in range(per):
            inner_re, inner_im = (
                jnp.where(
                    first_slot,
                    dot(grouped[p], right_side[target, 0, side]),
                    dot(grouped[p], right_side[target, 1, side]),
                )
                for side in range(2)
            )
            outer_re = spread[target, 0, p]
            outer_im = spread[target, 1, p]
            real = real + fold(outer_re * inner_re - outer_im * inner_im)
            imag = imag + fold(outer_re * inner_im + outer_im * inner_re)
        return jnp.concatenate([real, imag], axis=0)

    def give(side):
        return pltpu.make_async_remote_copy(
            src_ref=halo_out.at[side],
            dst_ref=halo_in.at[1 - side],
            send_sem=halo_send.at[side],
            recv_sem=halo_recv.at[1 - side],
            device_id={"rows": lax.rem(row + n_r - 1 + 2 * side, n_r)},
            device_id_type=MESH,
        )

    @pl.when(jnp.logical_not(has_left))
    def _():
        halo_in[0] = jnp.zeros(halo_in.shape[1:], jnp.float32)

    @pl.when(jnp.logical_not(has_right))
    def _():
        halo_in[1] = jnp.zeros(halo_in.shape[1:], jnp.float32)

    @pl.loop(0, 2)
    def _(turn):
        side = lax.rem(row + turn, 2)

        @pl.when(jnp.logical_or(jnp.logical_and(side == 0, has_left), jnp.logical_and(side == 1, has_right)))
        def _():
            halo_out[side] = contribution(side, rows_two)
            give(side).start()

    density = contribution(2, rows_two)
    direct = [jnp.zeros((4, LANES), jnp.float32), jnp.zeros((4, LANES), jnp.float32)]
    shape = (lines, LANES)
    for p in range(per):
        on_diagonal = iota(shape, 1) == iota(shape, 0) // 4 * per + p
        for c in range(2):
            entries = rows_two[p, :, c * LANES : (c + 1) * LANES].astype(jnp.float32)
            direct[c] = direct[c] + fold(jnp.where(on_diagonal, entries, 0.0))
    shape = (LANES, width)
    place = iota(shape, 1) == iota(shape, 0) + start[0]
    density = density + dot(
        jnp.concatenate(direct, axis=0).astype(jnp.bfloat16), place.astype(jnp.bfloat16)
    )

    @pl.when(is_far)
    def _():
        @pl.loop(0, n_e)
        def _(step):
            cross(step, step).wait_recv()

        regroup(land_far, rows_far)
        halo_in[far_side] = contribution(far_side, rows_far)

    @pl.loop(1, n_e)
    def _(step):
        exchange(*two, lax.rem(me + step, n_e)).wait_send()

    @pl.when(is_far)
    def _():
        @pl.loop(0, n_e)
        def _(step):
            cross(step, me).wait_send()

    @pl.when(has_right)
    def _():
        to_right.wait_send()
        give(1).wait_send()

    @pl.when(has_left)
    def _():
        to_left.wait_send()
        give(0).wait_send()

    @pl.when(has_left)
    def _():
        give(1).wait_recv()

    @pl.when(has_right)
    def _():
        give(0).wait_recv()

    density = density + halo_in[0] + halo_in[1]
    for c in range(2):
        for g in range(2):
            out[g, c] = density[4 * c + 2 * g : 4 * c + 2 * g + 2]


def shards(green_window, screened, retarded, energy_order, window_start):
    n_e = lax.axis_size("energy")
    entries = green_window.shape[4]
    columns = screened.shape[4]
    total = screened.shape[2]
    slab, width = retarded.shape[4], retarded.shape[5]
    per = slab // n_e
    half = jnp.bfloat16
    full = jnp.float32
    lines = 4 * n_e
    scratch = [
        pltpu.VMEM((4, 2, entries), half),
        pltpu.VMEM((4, total, columns), half),
        pltpu.VMEM((2, 2, slab, width), half),
        pltpu.VMEM((1, total), jnp.int32),
        pltpu.VMEM((4, total, 4 * total), half),
        pltpu.VMEM((8, entries), full),
        pltpu.VMEM((n_e, 8, per * LANES), half),
        pltpu.VMEM((n_e, 8, per * LANES), half),
        pltpu.VMEM((4 * total, per * LANES), full),
        pltpu.VMEM((8 * total, 4 * total), half),
        pltpu.VMEM((8 * total, 4 * total), half),
        pltpu.VMEM((n_e, 4, 2 * per * LANES), half),
        pltpu.VMEM((n_e, 4, 2 * per * LANES), half),
        pltpu.VMEM((per, lines, 2 * LANES), half),
        pltpu.VMEM((n_e, 4, 2 * per * LANES), half),
        pltpu.VMEM((per, lines, 2 * LANES), half),
        pltpu.VMEM((2, 2, slab, width), half),
        pltpu.VMEM((2, 2, slab, width), half),
        pltpu.VMEM((2, 2, slab, width), half),
        pltpu.VMEM((3, 2, 2, 2 * LANES, width), half),
        pltpu.VMEM((3, 2, per, lines, width), full),
        pltpu.VMEM((2, 8, width), full),
        pltpu.VMEM((2, 8, width), full),
        pltpu.SemaphoreType.DMA((7,)),
        pltpu.SemaphoreType.DMA((n_e,)),
        pltpu.SemaphoreType.DMA((n_e,)),
        pltpu.SemaphoreType.DMA((n_e,)),
        pltpu.SemaphoreType.DMA((n_e,)),
        pltpu.SemaphoreType.DMA((n_e,)),
        pltpu.SemaphoreType.DMA((n_e,)),
        pltpu.SemaphoreType.DMA((2,)),
        pltpu.SemaphoreType.DMA((2,)),
        pltpu.SemaphoreType.DMA((2,)),
        pltpu.SemaphoreType.DMA((2,)),
    ]
    anywhere = pl.BlockSpec(memory_space=pltpu.HBM)
    density = pl.pallas_call(
        kernel,
        out_shape=jax.ShapeDtypeStruct((2, 2, 2, width), full),
        in_specs=[anywhere] * 5 + [pl.BlockSpec(memory_space=pltpu.SMEM)],
        out_specs=pl.BlockSpec(memory_space=pltpu.VMEM),
        scratch_shapes=scratch,
        compiler_params=pltpu.CompilerParams(
            collective_id=0, has_side_effects=True, vmem_limit_bytes=48 * 2**20
        ),
    )(
        *[
            pltpu.with_memory_space_constraint(array, pltpu.HBM)
            for array in (
                green_window.reshape(4, 2, entries),
                screened.reshape(4, total, columns),
                retarded[:, :, 0],
                energy_order.reshape(1, total),
                jnp.asarray(phase_tables(total)),
            )
        ],
        window_start,
    )
    return density[:, :, :, None, :]


def solution(mesh):
    in_specs = (
        P(None, None, "energy", "rows", None),
        P(None, None, None, "rows", "energy"),
        P(None, "energy", "rows", None, None, None),
        P(),
        P("rows"),
    )
    out_specs = P(None, None, "energy", "rows", None)
    return jax.shard_map(shards, mesh=mesh, in_specs=in_specs, out_specs=out_specs, check_vma=False)
```

```python
import functools
import math

import jax
import jax.numpy as jnp
import numpy as np
from jax import lax
from jax.experimental import pallas as pl
from jax.experimental.pallas import tpu as pltpu
from jax.sharding import PartitionSpec as P

MESH = pl.DeviceIdType.MESH
PLANES = 8
LANES = 128


def phase_tables(total):
    turns = np.outer(np.arange(total), np.arange(total)) % total
    angle = 2.0 * math.pi / total * turns
    parts = []
    for exact in (np.cos(angle), np.sin(angle)):
        high = exact.astype(jnp.bfloat16)
        low = (exact - high.astype(np.float64)).astype(jnp.bfloat16)
        parts.append((high, low))
    stacked = np.stack([parts[0][0], parts[1][0], parts[0][1], parts[1][1]])
    return np.tile(stacked, (1, 1, 4))


def dot(left, right):
    return jnp.dot(left, right, preferred_element_type=jnp.float32)


def iota(shape, axis):
    return lax.broadcasted_iota(jnp.int32, shape, axis)


def kernel(
    green, screened, retarded, order, tables, start, out,
    green_v, screen_v, own_v, order_v, tables_v,
    flat, chunks, land_one, weights, forward, backward,
    chunks_two, land_two, rows_two, land_far, rows_far, far_v, from_left, from_right, right_side, spread, halo_out, halo_in,
    local_sem, send_one, recv_one, send_two, recv_two, send_far, recv_far, ret_send, ret_recv, halo_send, halo_recv,
):
    n_e = lax.axis_size("energy")
    n_r = lax.axis_size("rows")
    me = lax.axis_index("energy")
    row = lax.axis_index("rows")
    slab, width = own_v.shape[2], own_v.shape[3]
    total = order_v.shape[1]
    per = slab // n_e
    middle = n_r // 2
    far_row = 2 * middle - 1 - row
    far_side = middle - row
    is_far = jnp.logical_or(row == middle - 1, row == middle)
    has_left = jnp.logical_and(row > 0, row != middle)
    has_right = jnp.logical_and(row < n_r - 1, row != middle - 1)

    plane = max(1, n_e // PLANES)
    planes = n_e // plane

    def far_first(step):
        turn = step // plane
        shift = planes // 2 + (turn + 1) // 2 * (1 - 2 * lax.rem(turn, 2))
        return lax.rem(me // plane + shift, planes) * plane + lax.rem(me + step, plane)

    barrier = pltpu.get_barrier_semaphore()

    @pl.loop(0, n_e)
    def _(step):
        other = far_first(step)

        @pl.when(other != me)
        def _():
            pl.semaphore_signal(barrier, inc=1, device_id={"energy": other}, device_id_type=MESH)

    @pl.when(row > 0)
    def _():
        pl.semaphore_signal(barrier, inc=1, device_id={"rows": row - 1}, device_id_type=MESH)

    @pl.when(row < n_r - 1)
    def _():
        pl.semaphore_signal(barrier, inc=1, device_id={"rows": row + 1}, device_id_type=MESH)

    halo_out[...] = jnp.zeros_like(halo_out)

    loads = [
        pltpu.make_async_copy(green, green_v, local_sem.at[0]),
        pltpu.make_async_copy(order, order_v, local_sem.at[1]),
        pltpu.make_async_copy(tables, tables_v, local_sem.at[2]),
        pltpu.make_async_copy(screened, screen_v, local_sem.at[3]),
        pltpu.make_async_copy(retarded.at[:, :, 1], own_v, local_sem.at[4]),
    ]
    for load in loads:
        load.start()
    far_load = pltpu.make_async_copy(retarded.at[:, :, 2 * far_side], far_v, local_sem.at[6])

    @pl.when(is_far)
    def _():
        far_load.start()

    loads[0].wait()
    for pair in range(4):
        flat[2 * pair : 2 * pair + 2, :] = green_v[pair].astype(jnp.float32)
    group = n_e
    for size in (1, 2, 4, 8, 16):
        if size < n_e and n_e % size == 0 and size * per * slab % LANES == 0:
            group = size
            break
    margin = jnp.zeros((8, LANES - slab), jnp.float32)

    @pl.loop(0, n_e // group)
    def _(step):
        window = group * per * slab
        if group == n_e:
            cut = flat[...]
        else:
            cut = flat[:, pl.ds(pl.multiple_of(step * window, LANES), window)]
        for place in range(group * per):
            piece = cut[:, place * slab : (place + 1) * slab]
            lane = place % per * LANES
            chunks[step * group + place // per, :, lane : lane + LANES] = jnp.concatenate(
                [piece, margin], axis=1
            ).astype(jnp.bfloat16)

    beside = (row + n_r - 1) // n_r + (2 * n_r - 2 - row) // n_r
    pl.semaphore_wait(barrier, n_e - 1 + beside)

    def exchange(source, target, send_sem, recv_sem, other):
        return pltpu.make_async_remote_copy(
            src_ref=source.at[other],
            dst_ref=target.at[me],
            send_sem=send_sem.at[other],
            recv_sem=recv_sem.at[me],
            device_id={"energy": other},
            device_id_type=MESH,
        )

    def arrival(source, target, send_sem, recv_sem, other):
        return pltpu.make_async_remote_copy(
            src_ref=source.at[other],
            dst_ref=target.at[other],
            send_sem=send_sem.at[other],
            recv_sem=recv_sem.at[other],
            device_id={"energy": other},
            device_id_type=MESH,
        )

    def cross(step, device):
        return pltpu.make_async_remote_copy(
            src_ref=chunks_two.at[step],
            dst_ref=land_far.at[device],
            send_sem=send_far.at[step],
            recv_sem=recv_far.at[device],
            device_id={"energy": step, "rows": far_row},
            device_id_type=MESH,
        )

    one = (chunks, land_one, send_one, recv_one)
    two = (chunks_two, land_two, send_two, recv_two)

    @pl.loop(0, n_e)
    def _(step):
        other = far_first(step)

        @pl.when(other != me)
        def _():
            exchange(*one, other).start()

    to_right = pltpu.make_async_remote_copy(
        src_ref=retarded.at[:, :, 2], dst_ref=from_left, send_sem=ret_send.at[0], recv_sem=ret_recv.at[0],
        device_id={"rows": lax.rem(row + 1, n_r)}, device_id_type=MESH,
    )
    to_left = pltpu.make_async_remote_copy(
        src_ref=retarded.at[:, :, 0], dst_ref=from_right, send_sem=ret_send.at[1], recv_sem=ret_recv.at[1],
        device_id={"rows": lax.rem(row + n_r - 1, n_r)}, device_id_type=MESH,
    )

    @pl.when(has_right)
    def _():
        to_right.start()

    @pl.when(has_left)
    def _():
        to_left.start()

    land_one[me] = chunks[me]

    loads[1].wait()
    loads[2].wait()
    count = 4 * total
    energies = (iota((total, total), 0) == order_v[...]).astype(jnp.bfloat16)
    column = iota((total, count), 1)
    slot_of_column = column // 8 * 2 + column % 2
    pick = (iota((total, count), 0) == slot_of_column).astype(jnp.bfloat16)
    hot = dot(energies, pick).astype(jnp.bfloat16)
    shape = (total, count)
    col = iota(shape, 1)
    col_g, col_c = col // 4 % 2, col // 2 % 2
    for part in range(2):
        cosine = dot(tables_v[2 * part, :, :total], hot)
        sine = dot(tables_v[2 * part + 1, :, :total], hot)
        for g in range(2):
            real = jnp.where(col_c == 0, cosine, sine)
            imag = jnp.where(col_c == 0, -sine, cosine)
            base = part * count + g * 2 * total
            forward[base : base + total, :] = jnp.where(col_g == g, real, 0.0).astype(jnp.bfloat16)
            forward[base + total : base + 2 * total, :] = jnp.where(col_g == g, imag, 0.0).astype(jnp.bfloat16)
    half = 2 * total
    line = iota((half, total), 0)
    slot_of_line = line // 4 * 2 + line % 2
    pick_line = (iota((half, total), 1) == slot_of_line).astype(jnp.bfloat16)
    hot_line = lax.dot_general(
        pick_line, energies, (((1,), (1,)), ((), ())), preferred_element_type=jnp.float32
    ).astype(jnp.bfloat16)
    shape = (half, count)
    same_g = iota(shape, 0) // 2 % 2 == iota(shape, 1) // (2 * total)
    from_real = iota(shape, 1) // total % 2 == 0
    scale = 1.0 / total
    for part in range(2):
        cosine = dot(hot_line, tables_v[2 * part]) * scale
        sine = dot(hot_line, tables_v[2 * part + 1]) * scale
        real = jnp.where(from_real, -sine, -cosine)
        imag = jnp.where(from_real, cosine, -sine)
        base = part * count
        backward[base : base + half, :] = jnp.where(same_g, real, 0.0).astype(jnp.bfloat16)
        backward[base + half : base + count, :] = jnp.where(same_g, imag, 0.0).astype(jnp.bfloat16)

    loads[3].wait()
    screen_margin = jnp.zeros((total, LANES - slab), jnp.float32)
    for pair in range(4):
        entries = screen_v[pair].astype(jnp.float32)
        for p in range(per):
            weights[pair * total : (pair + 1) * total, p * LANES : (p + 1) * LANES] = jnp.concatenate(
                [entries[:, p * slab : (p + 1) * slab], screen_margin], axis=1
            )

    lines = 4 * n_e
    line = iota((lines, slab), 0)
    orbital = iota((lines, slab), 1)
    blank = jnp.zeros((LANES - slab, width), jnp.bfloat16)

    def prepare(block, target):
        for slot in range(2):
            real = block[0, slot]
            imag = block[1, slot]
            for side, (upper, lower) in enumerate(((real, imag), (-imag, real))):
                right_side[target, slot, side, 0:slab] = upper
                right_side[target, slot, side, slab:LANES] = blank
                right_side[target, slot, side, LANES : LANES + slab] = lower
                right_side[target, slot, side, LANES + slab :] = blank
            for p in range(per):
                chosen = jnp.where(line % 2 == slot, line // 4 * per + p, -1)
                select = (orbital == chosen).astype(jnp.bfloat16)
                for part, values in enumerate((real, imag)):
                    rows = dot(select, values)
                    spread[target, part, p] = rows if slot == 0 else spread[target, part, p] + rows

    loads[4].wait()
    prepare(own_v, 2)

    @pl.when(is_far)
    def _():
        far_load.wait()
        prepare(far_v, far_side)

    @pl.loop(1, n_e)
    def _(step):
        arrival(*one, lax.rem(me + step, n_e)).wait_recv()

    arrived = land_one[...].reshape(8 * n_e, per * LANES)
    times = dot(forward[...], arrived)
    times = times[:count] + times[count:]
    mixed = []
    for g in range(2):
        base = g * 2 * total
        green_re, green_im = times[base : base + total], times[base + total : base + 2 * total]
        screen_re, screen_im = weights[base : base + total], weights[base + total : base + 2 * total]
        mixed.append(green_re * screen_re - green_im * screen_im)
        mixed.append(green_re * screen_im + green_im * screen_re)
    mixed = jnp.concatenate(mixed, axis=0)
    high = mixed.astype(jnp.bfloat16)
    low = (mixed - high.astype(jnp.float32)).astype(jnp.bfloat16)
    first = dot(backward[...], high)
    sigma = first[:count] + (first[count:] + dot(backward[0:count], low))
    sigma = sigma.astype(jnp.bfloat16)
    for c in range(2):
        for p in range(per):
            lane = (2 * p + c) * LANES
            chunks_two[:, :, lane : lane + LANES] = sigma[
                c * half : (c + 1) * half, p * LANES : (p + 1) * LANES
            ].reshape(n_e, 4, LANES)

    @pl.loop(0, n_e)
    def _(step):
        other = step // plane * plane + lax.rem(me + step, plane)

        @pl.when(other != me)
        def _():
            exchange(*two, other).start()

    @pl.when(is_far)
    def _():
        @pl.loop(0, n_e)
        def _(step):
            cross(step // plane * plane + lax.rem(me + step, plane), me).start()

    land_two[me] = chunks_two[me]

    @pl.when(has_left)
    def _():
        to_right.wait_recv()
        prepare(from_left, 0)

    @pl.when(has_right)
    def _():
        to_left.wait_recv()
        prepare(from_right, 1)

    @pl.loop(1, n_e)
    def _(step):
        exchange(*one, lax.rem(me + step, n_e)).wait_send()

    @pl.loop(1, n_e)
    def _(step):
        arrival(*two, lax.rem(me + step, n_e)).wait_recv()

    def regroup(landed, grouped):
        for p in range(per):
            grouped[p] = landed[:, :, 2 * p * LANES : 2 * (p + 1) * LANES].reshape(lines, 2 * LANES)

    regroup(land_two, rows_two)

    def fold(values):
        values = values.reshape(lines // 8, 8, values.shape[1]).sum(axis=0)
        return values[0:4] + values[4:8]

    first_slot = iota((lines, width), 0) % 2 == 0

    def contribution(target, grouped):
        real = jnp.zeros((4, width), jnp.float32)
        imag = jnp.zeros((4, width), jnp.float32)
        for p in range(per):
            inner_re, inner_im = (
                jnp.where(
                    first_slot,
                    dot(grouped[p], right_side[target, 0, side]),
                    dot(grouped[p], right_side[target, 1, side]),
                )
                for side in range(2)
            )
            outer_re = spread[target, 0, p]
            outer_im = spread[target, 1, p]
            real = real + fold(outer_re * inner_re - outer_im * inner_im)
            imag = imag + fold(outer_re * inner_im + outer_im * inner_re)
        return jnp.concatenate([real, imag], axis=0)

    def give(side):
        return pltpu.make_async_remote_copy(
            src_ref=halo_out.at[side],
            dst_ref=halo_in.at[1 - side],
            send_sem=halo_send.at[side],
            recv_sem=halo_recv.at[1 - side],
            device_id={"rows": lax.rem(row + n_r - 1 + 2 * side, n_r)},
            device_id_type=MESH,
        )

    @pl.when(jnp.logical_not(has_left))
    def _():
        halo_in[0] = jnp.zeros(halo_in.shape[1:], jnp.float32)

    @pl.when(jnp.logical_not(has_right))
    def _():
        halo_in[1] = jnp.zeros(halo_in.shape[1:], jnp.float32)

    @pl.loop(0, 2)
    def _(turn):
        side = lax.rem(row + turn, 2)

        @pl.when(jnp.logical_or(jnp.logical_and(side == 0, has_left), jnp.logical_and(side == 1, has_right)))
        def _():
            halo_out[side, :, :width] = contribution(side, rows_two)
            give(side).start()

    density = contribution(2, rows_two)
    direct = [jnp.zeros((4, LANES), jnp.float32), jnp.zeros((4, LANES), jnp.float32)]
    shape = (lines, LANES)
    for p in range(per):
        on_diagonal = iota(shape, 1) == iota(shape, 0) // 4 * per + p
        for c in range(2):
            entries = rows_two[p, :, c * LANES : (c + 1) * LANES].astype(jnp.float32)
            direct[c] = direct[c] + fold(jnp.where(on_diagonal, entries, 0.0))
    shape = (LANES, width)
    place = iota(shape, 1) == iota(shape, 0) + start[0]
    density = density + dot(
        jnp.concatenate(direct, axis=0).astype(jnp.bfloat16), place.astype(jnp.bfloat16)
    )

    @pl.when(is_far)
    def _():
        @pl.loop(0, n_e)
        def _(step):
            cross(step, step).wait_recv()

        regroup(land_far, rows_far)
        halo_in[far_side, :, :width] = contribution(far_side, rows_far)

    @pl.loop(1, n_e)
    def _(step):
        exchange(*two, lax.rem(me + step, n_e)).wait_send()

    @pl.when(is_far)
    def _():
        @pl.loop(0, n_e)
        def _(step):
            cross(step, me).wait_send()

    @pl.when(has_right)
    def _():
        to_right.wait_send()
        give(1).wait_send()

    @pl.when(has_left)
    def _():
        to_left.wait_send()
        give(0).wait_send()

    @pl.when(has_left)
    def _():
        give(1).wait_recv()

    @pl.when(has_right)
    def _():
        give(0).wait_recv()

    density = density + halo_in[0, :, :width] + halo_in[1, :, :width]
    for c in range(2):
        for g in range(2):
            out[g, c] = density[4 * c + 2 * g : 4 * c + 2 * g + 2]


def shards(green_window, screened, retarded, energy_order, window_start):
    n_e = lax.axis_size("energy")
    entries = green_window.shape[4]
    columns = screened.shape[4]
    total = screened.shape[2]
    slab, width = retarded.shape[4], retarded.shape[5]
    per = slab // n_e
    half = jnp.bfloat16
    full = jnp.float32
    lines = 4 * n_e
    padded = pl.cdiv(width, LANES) * LANES
    scratch = [
        pltpu.VMEM((4, 2, entries), half),
        pltpu.VMEM((4, total, columns), half),
        pltpu.VMEM((2, 2, slab, width), half),
        pltpu.VMEM((1, total), jnp.int32),
        pltpu.VMEM((4, total, 4 * total), half),
        pltpu.VMEM((8, entries), full),
        pltpu.VMEM((n_e, 8, per * LANES), half),
        pltpu.VMEM((n_e, 8, per * LANES), half),
        pltpu.VMEM((4 * total, per * LANES), full),
        pltpu.VMEM((8 * total, 4 * total), half),
        pltpu.VMEM((8 * total, 4 * total), half),
        pltpu.VMEM((n_e, 4, 2 * per * LANES), half),
        pltpu.VMEM((n_e, 4, 2 * per * LANES), half),
        pltpu.VMEM((per, lines, 2 * LANES), half),
        pltpu.VMEM((n_e, 4, 2 * per * LANES), half),
        pltpu.VMEM((per, lines, 2 * LANES), half),
        pltpu.VMEM((2, 2, slab, width), half),
        pltpu.VMEM((2, 2, slab, width), half),
        pltpu.VMEM((2, 2, slab, width), half),
        pltpu.VMEM((3, 2, 2, 2 * LANES, width), half),
        pltpu.VMEM((3, 2, per, lines, width), full),
        pltpu.VMEM((2, 8, padded), full),
        pltpu.VMEM((2, 8, padded), full),
        pltpu.SemaphoreType.DMA((7,)),
        pltpu.SemaphoreType.DMA((n_e,)),
        pltpu.SemaphoreType.DMA((n_e,)),
        pltpu.SemaphoreType.DMA((n_e,)),
        pltpu.SemaphoreType.DMA((n_e,)),
        pltpu.SemaphoreType.DMA((n_e,)),
        pltpu.SemaphoreType.DMA((n_e,)),
        pltpu.SemaphoreType.DMA((2,)),
        pltpu.SemaphoreType.DMA((2,)),
        pltpu.SemaphoreType.DMA((2,)),
        pltpu.SemaphoreType.DMA((2,)),
    ]
    anywhere = pl.BlockSpec(memory_space=pltpu.HBM)
    density = pl.pallas_call(
        kernel,
        out_shape=jax.ShapeDtypeStruct((2, 2, 2, width), full),
        in_specs=[anywhere] * 5 + [pl.BlockSpec(memory_space=pltpu.SMEM)],
        out_specs=pl.BlockSpec(memory_space=pltpu.VMEM),
        scratch_shapes=scratch,
        compiler_params=pltpu.CompilerParams(
            collective_id=0, has_side_effects=True, vmem_limit_bytes=48 * 2**20
        ),
    )(
        *[
            pltpu.with_memory_space_constraint(array, pltpu.HBM)
            for array in (
                green_window.reshape(4, 2, entries),
                screened.reshape(4, total, columns),
                retarded[:, :, 0],
                energy_order.reshape(1, total),
                jnp.asarray(phase_tables(total)),
            )
        ],
        window_start,
    )
    return density[:, :, :, None, :]


def solution(mesh):
    in_specs = (
        P(None, None, "energy", "rows", None),
        P(None, None, None, "rows", "energy"),
        P(None, "energy", "rows", None, None, None),
        P(),
        P("rows"),
    )
    out_specs = P(None, None, "energy", "rows", None)
    return jax.shard_map(shards, mesh=mesh, in_specs=in_specs, out_specs=out_specs, check_vma=False)
```

```python
import functools
import math

import jax
import jax.numpy as jnp
import numpy as np
from jax import lax
from jax.experimental import pallas as pl
from jax.experimental.pallas import tpu as pltpu
from jax.sharding import PartitionSpec as P

MESH = pl.DeviceIdType.MESH
PLANES = 8
LANES = 128


def phase_tables(total):
    turns = np.outer(np.arange(total), np.arange(total)) % total
    angle = 2.0 * math.pi / total * turns
    parts = []
    for exact in (np.cos(angle), np.sin(angle)):
        high = exact.astype(jnp.bfloat16)
        low = (exact - high.astype(np.float64)).astype(jnp.bfloat16)
        parts.append((high, low))
    stacked = np.stack([parts[0][0], parts[1][0], parts[0][1], parts[1][1]])
    return np.tile(stacked, (1, 1, 4))


def dot(left, right):
    return jnp.dot(left, right, preferred_element_type=jnp.float32)


def iota(shape, axis):
    return lax.broadcasted_iota(jnp.int32, shape, axis)


def kernel(
    green, screened, retarded, order, tables, start, out,
    green_v, screen_v, own_v, order_v, tables_v,
    flat, chunks, land_one, weights, forward, backward,
    chunks_two, land_two, rows_two, land_far, rows_far, far_v, from_left, from_right, right_side, spread, halo_out, halo_in,
    local_sem, send_one, recv_one, send_two, recv_two, send_far, recv_far, ret_send, ret_recv, halo_send, halo_recv,
):
    n_e = lax.axis_size("energy")
    n_r = lax.axis_size("rows")
    me = lax.axis_index("energy")
    row = lax.axis_index("rows")
    slab, width = own_v.shape[2], own_v.shape[3]
    total = order_v.shape[1]
    per = slab // n_e
    middle = n_r // 2
    far_row = 2 * middle - 1 - row
    far_side = middle - row
    is_far = jnp.logical_or(row == middle - 1, row == middle)
    has_left = jnp.logical_and(row > 0, row != middle)
    has_right = jnp.logical_and(row < n_r - 1, row != middle - 1)

    plane = max(1, n_e // PLANES)
    planes = n_e // plane

    def far_first(step):
        turn = step // plane
        shift = planes // 2 + (turn + 1) // 2 * (1 - 2 * lax.rem(turn + row, 2))
        return lax.rem(me // plane + shift, planes) * plane + lax.rem(me + step, plane)

    barrier = pltpu.get_barrier_semaphore()

    @pl.loop(0, n_e)
    def _(step):
        other = far_first(step)

        @pl.when(other != me)
        def _():
            pl.semaphore_signal(barrier, inc=1, device_id={"energy": other}, device_id_type=MESH)

    @pl.when(row > 0)
    def _():
        pl.semaphore_signal(barrier, inc=1, device_id={"rows": row - 1}, device_id_type=MESH)

    @pl.when(row < n_r - 1)
    def _():
        pl.semaphore_signal(barrier, inc=1, device_id={"rows": row + 1}, device_id_type=MESH)

    halo_out[...] = jnp.zeros_like(halo_out)

    loads = [
        pltpu.make_async_copy(green, green_v, local_sem.at[0]),
        pltpu.make_async_copy(order, order_v, local_sem.at[1]),
        pltpu.make_async_copy(tables, tables_v, local_sem.at[2]),
        pltpu.make_async_copy(screened, screen_v, local_sem.at[3]),
        pltpu.make_async_copy(retarded.at[:, :, 1], own_v, local_sem.at[4]),
    ]
    for load in loads:
        load.start()
    far_load = pltpu.make_async_copy(retarded.at[:, :, 2 * far_side], far_v, local_sem.at[6])

    @pl.when(is_far)
    def _():
        far_load.start()

    loads[0].wait()
    for pair in range(4):
        flat[2 * pair : 2 * pair + 2, :] = green_v[pair].astype(jnp.float32)
    group = n_e
    for size in (1, 2, 4, 8, 16):
        if size < n_e and n_e % size == 0 and size * per * slab % LANES == 0:
            group = size
            break
    margin = jnp.zeros((8, LANES - slab), jnp.float32)

    @pl.loop(0, n_e // group)
    def _(step):
        window = group * per * slab
        if group == n_e:
            cut = flat[...]
        else:
            cut = flat[:, pl.ds(pl.multiple_of(step * window, LANES), window)]
        for place in range(group * per):
            piece = cut[:, place * slab : (place + 1) * slab]
            lane = place % per * LANES
            chunks[step * group + place // per, :, lane : lane + LANES] = jnp.concatenate(
                [piece, margin], axis=1
            ).astype(jnp.bfloat16)

    beside = (row + n_r - 1) // n_r + (2 * n_r - 2 - row) // n_r
    pl.semaphore_wait(barrier, n_e - 1 + beside)

    def exchange(source, target, send_sem, recv_sem, other):
        return pltpu.make_async_remote_copy(
            src_ref=source.at[other],
            dst_ref=target.at[me],
            send_sem=send_sem.at[other],
            recv_sem=recv_sem.at[me],
            device_id={"energy": other},
            device_id_type=MESH,
        )

    def arrival(source, target, send_sem, recv_sem, other):
        return pltpu.make_async_remote_copy(
            src_ref=source.at[other],
            dst_ref=target.at[other],
            send_sem=send_sem.at[other],
            recv_sem=recv_sem.at[other],
            device_id={"energy": other},
            device_id_type=MESH,
        )

    def cross(step, device):
        return pltpu.make_async_remote_copy(
            src_ref=chunks_two.at[step],
            dst_ref=land_far.at[device],
            send_sem=send_far.at[step],
            recv_sem=recv_far.at[device],
            device_id={"energy": step, "rows": far_row},
            device_id_type=MESH,
        )

    one = (chunks, land_one, send_one, recv_one)
    two = (chunks_two, land_two, send_two, recv_two)

    @pl.loop(0, n_e)
    def _(step):
        other = far_first(step)

        @pl.when(other != me)
        def _():
            exchange(*one, other).start()

    to_right = pltpu.make_async_remote_copy(
        src_ref=retarded.at[:, :, 2], dst_ref=from_left, send_sem=ret_send.at[0], recv_sem=ret_recv.at[0],
        device_id={"rows": lax.rem(row + 1, n_r)}, device_id_type=MESH,
    )
    to_left = pltpu.make_async_remote_copy(
        src_ref=retarded.at[:, :, 0], dst_ref=from_right, send_sem=ret_send.at[1], recv_sem=ret_recv.at[1],
        device_id={"rows": lax.rem(row + n_r - 1, n_r)}, device_id_type=MESH,
    )

    @pl.when(has_right)
    def _():
        to_right.start()

    @pl.when(has_left)
    def _():
        to_left.start()

    land_one[me] = chunks[me]

    loads[1].wait()
    loads[2].wait()
    count = 4 * total
    energies = (iota((total, total), 0) == order_v[...]).astype(jnp.bfloat16)
    column = iota((total, count), 1)
    slot_of_column = column // 8 * 2 + column % 2
    pick = (iota((total, count), 0) == slot_of_column).astype(jnp.bfloat16)
    hot = dot(energies, pick).astype(jnp.bfloat16)
    shape = (total, count)
    col = iota(shape, 1)
    col_g, col_c = col // 4 % 2, col // 2 % 2
    for part in range(2):
        cosine = dot(tables_v[2 * part, :, :total], hot)
        sine = dot(tables_v[2 * part + 1, :, :total], hot)
        for g in range(2):
            real = jnp.where(col_c == 0, cosine, sine)
            imag = jnp.where(col_c == 0, -sine, cosine)
            base = part * count + g * 2 * total
            forward[base : base + total, :] = jnp.where(col_g == g, real, 0.0).astype(jnp.bfloat16)
            forward[base + total : base + 2 * total, :] = jnp.where(col_g == g, imag, 0.0).astype(jnp.bfloat16)
    half = 2 * total
    line = iota((half, total), 0)
    slot_of_line = line // 4 * 2 + line % 2
    pick_line = (iota((half, total), 1) == slot_of_line).astype(jnp.bfloat16)
    hot_line = lax.dot_general(
        pick_line, energies, (((1,), (1,)), ((), ())), preferred_element_type=jnp.float32
    ).astype(jnp.bfloat16)
    shape = (half, count)
    same_g = iota(shape, 0) // 2 % 2 == iota(shape, 1) // (2 * total)
    from_real = iota(shape, 1) // total % 2 == 0
    scale = 1.0 / total
    for part in range(2):
        cosine = dot(hot_line, tables_v[2 * part]) * scale
        sine = dot(hot_line, tables_v[2 * part + 1]) * scale
        real = jnp.where(from_real, -sine, -cosine)
        imag = jnp.where(from_real, cosine, -sine)
        base = part * count
        backward[base : base + half, :] = jnp.where(same_g, real, 0.0).astype(jnp.bfloat16)
        backward[base + half : base + count, :] = jnp.where(same_g, imag, 0.0).astype(jnp.bfloat16)

    loads[3].wait()
    screen_margin = jnp.zeros((total, LANES - slab), jnp.float32)
    for pair in range(4):
        entries = screen_v[pair].astype(jnp.float32)
        for p in range(per):
            weights[pair * total : (pair + 1) * total, p * LANES : (p + 1) * LANES] = jnp.concatenate(
                [entries[:, p * slab : (p + 1) * slab], screen_margin], axis=1
            )

    lines = 4 * n_e
    line = iota((lines, slab), 0)
    orbital = iota((lines, slab), 1)
    blank = jnp.zeros((LANES - slab, width), jnp.bfloat16)

    def prepare(block, target):
        for slot in range(2):
            real = block[0, slot]
            imag = block[1, slot]
            for side, (upper, lower) in enumerate(((real, imag), (-imag, real))):
                right_side[target, slot, side, 0:slab] = upper
                right_side[target, slot, side, slab:LANES] = blank
                right_side[target, slot, side, LANES : LANES + slab] = lower
                right_side[target, slot, side, LANES + slab :] = blank
            for p in range(per):
                chosen = jnp.where(line % 2 == slot, line // 4 * per + p, -1)
                select = (orbital == chosen).astype(jnp.bfloat16)
                for part, values in enumerate((real, imag)):
                    rows = dot(select, values)
                    spread[target, part, p] = rows if slot == 0 else spread[target, part, p] + rows

    loads[4].wait()
    prepare(own_v, 2)

    @pl.when(is_far)
    def _():
        far_load.wait()
        prepare(far_v, far_side)

    @pl.loop(1, n_e)
    def _(step):
        arrival(*one, lax.rem(me + step, n_e)).wait_recv()

    arrived = land_one[...].reshape(8 * n_e, per * LANES)
    times = dot(forward[...], arrived)
    times = times[:count] + times[count:]
    mixed = []
    for g in range(2):
        base = g * 2 * total
        green_re, green_im = times[base : base + total], times[base + total : base + 2 * total]
        screen_re, screen_im = weights[base : base + total], weights[base + total : base + 2 * total]
        mixed.append(green_re * screen_re - green_im * screen_im)
        mixed.append(green_re * screen_im + green_im * screen_re)
    mixed = jnp.concatenate(mixed, axis=0)
    high = mixed.astype(jnp.bfloat16)
    low = (mixed - high.astype(jnp.float32)).astype(jnp.bfloat16)
    first = dot(backward[...], high)
    sigma = first[:count] + (first[count:] + dot(backward[0:count], low))
    sigma = sigma.astype(jnp.bfloat16)
    for c in range(2):
        for p in range(per):
            lane = (2 * p + c) * LANES
            chunks_two[:, :, lane : lane + LANES] = sigma[
                c * half : (c + 1) * half, p * LANES : (p + 1) * LANES
            ].reshape(n_e, 4, LANES)

    @pl.loop(0, n_e)
    def _(step):
        other = step // plane * plane + lax.rem(me + step, plane)

        @pl.when(other != me)
        def _():
            exchange(*two, other).start()

    @pl.when(is_far)
    def _():
        @pl.loop(0, n_e)
        def _(step):
            cross(step // plane * plane + lax.rem(me + step, plane), me).start()

    land_two[me] = chunks_two[me]

    @pl.when(has_left)
    def _():
        to_right.wait_recv()
        prepare(from_left, 0)

    @pl.when(has_right)
    def _():
        to_left.wait_recv()
        prepare(from_right, 1)

    @pl.loop(1, n_e)
    def _(step):
        exchange(*one, lax.rem(me + step, n_e)).wait_send()

    @pl.loop(1, n_e)
    def _(step):
        arrival(*two, lax.rem(me + step, n_e)).wait_recv()

    def regroup(landed, grouped):
        for p in range(per):
            grouped[p] = landed[:, :, 2 * p * LANES : 2 * (p + 1) * LANES].reshape(lines, 2 * LANES)

    regroup(land_two, rows_two)

    def fold(values):
        values = values.reshape(lines // 8, 8, values.shape[1]).sum(axis=0)
        return values[0:4] + values[4:8]

    first_slot = iota((lines, width), 0) % 2 == 0

    def contribution(target, grouped):
        real = jnp.zeros((4, width), jnp.float32)
        imag = jnp.zeros((4, width), jnp.float32)
        for p in range(per):
            inner_re, inner_im = (
                jnp.where(
                    first_slot,
                    dot(grouped[p], right_side[target, 0, side]),
                    dot(grouped[p], right_side[target, 1, side]),
                )
                for side in range(2)
            )
            outer_re = spread[target, 0, p]
            outer_im = spread[target, 1, p]
            real = real + fold(outer_re * inner_re - outer_im * inner_im)
            imag = imag + fold(outer_re * inner_im + outer_im * inner_re)
        return jnp.concatenate([real, imag], axis=0)

    def give(side):
        return pltpu.make_async_remote_copy(
            src_ref=halo_out.at[side],
            dst_ref=halo_in.at[1 - side],
            send_sem=halo_send.at[side],
            recv_sem=halo_recv.at[1 - side],
            device_id={"rows": lax.rem(row + n_r - 1 + 2 * side, n_r)},
            device_id_type=MESH,
        )

    @pl.when(jnp.logical_not(has_left))
    def _():
        halo_in[0] = jnp.zeros(halo_in.shape[1:], jnp.float32)

    @pl.when(jnp.logical_not(has_right))
    def _():
        halo_in[1] = jnp.zeros(halo_in.shape[1:], jnp.float32)

    @pl.loop(0, 2)
    def _(turn):
        side = lax.rem(row + turn, 2)

        @pl.when(jnp.logical_or(jnp.logical_and(side == 0, has_left), jnp.logical_and(side == 1, has_right)))
        def _():
            halo_out[side, :, :width] = contribution(side, rows_two)
            give(side).start()

    density = contribution(2, rows_two)
    direct = [jnp.zeros((4, LANES), jnp.float32), jnp.zeros((4, LANES), jnp.float32)]
    shape = (lines, LANES)
    for p in range(per):
        on_diagonal = iota(shape, 1) == iota(shape, 0) // 4 * per + p
        for c in range(2):
            entries = rows_two[p, :, c * LANES : (c + 1) * LANES].astype(jnp.float32)
            direct[c] = direct[c] + fold(jnp.where(on_diagonal, entries, 0.0))
    shape = (LANES, width)
    place = iota(shape, 1) == iota(shape, 0) + start[0]
    density = density + dot(
        jnp.concatenate(direct, axis=0).astype(jnp.bfloat16), place.astype(jnp.bfloat16)
    )

    @pl.when(is_far)
    def _():
        @pl.loop(0, n_e)
        def _(step):
            cross(step, step).wait_recv()

        regroup(land_far, rows_far)
        halo_in[far_side, :, :width] = contribution(far_side, rows_far)

    @pl.loop(1, n_e)
    def _(step):
        exchange(*two, lax.rem(me + step, n_e)).wait_send()

    @pl.when(is_far)
    def _():
        @pl.loop(0, n_e)
        def _(step):
            cross(step, me).wait_send()

    @pl.when(has_right)
    def _():
        to_right.wait_send()
        give(1).wait_send()

    @pl.when(has_left)
    def _():
        to_left.wait_send()
        give(0).wait_send()

    @pl.when(has_left)
    def _():
        give(1).wait_recv()

    @pl.when(has_right)
    def _():
        give(0).wait_recv()

    density = density + halo_in[0, :, :width] + halo_in[1, :, :width]
    for c in range(2):
        for g in range(2):
            out[g, c] = density[4 * c + 2 * g : 4 * c + 2 * g + 2]


def shards(green_window, screened, retarded, energy_order, window_start):
    n_e = lax.axis_size("energy")
    entries = green_window.shape[4]
    columns = screened.shape[4]
    total = screened.shape[2]
    slab, width = retarded.shape[4], retarded.shape[5]
    per = slab // n_e
    half = jnp.bfloat16
    full = jnp.float32
    lines = 4 * n_e
    padded = pl.cdiv(width, LANES) * LANES
    scratch = [
        pltpu.VMEM((4, 2, entries), half),
        pltpu.VMEM((4, total, columns), half),
        pltpu.VMEM((2, 2, slab, width), half),
        pltpu.VMEM((1, total), jnp.int32),
        pltpu.VMEM((4, total, 4 * total), half),
        pltpu.VMEM((8, entries), full),
        pltpu.VMEM((n_e, 8, per * LANES), half),
        pltpu.VMEM((n_e, 8, per * LANES), half),
        pltpu.VMEM((4 * total, per * LANES), full),
        pltpu.VMEM((8 * total, 4 * total), half),
        pltpu.VMEM((8 * total, 4 * total), half),
        pltpu.VMEM((n_e, 4, 2 * per * LANES), half),
        pltpu.VMEM((n_e, 4, 2 * per * LANES), half),
        pltpu.VMEM((per, lines, 2 * LANES), half),
        pltpu.VMEM((n_e, 4, 2 * per * LANES), half),
        pltpu.VMEM((per, lines, 2 * LANES), half),
        pltpu.VMEM((2, 2, slab, width), half),
        pltpu.VMEM((2, 2, slab, width), half),
        pltpu.VMEM((2, 2, slab, width), half),
        pltpu.VMEM((3, 2, 2, 2 * LANES, width), half),
        pltpu.VMEM((3, 2, per, lines, width), full),
        pltpu.VMEM((2, 8, padded), full),
        pltpu.VMEM((2, 8, padded), full),
        pltpu.SemaphoreType.DMA((7,)),
        pltpu.SemaphoreType.DMA((n_e,)),
        pltpu.SemaphoreType.DMA((n_e,)),
        pltpu.SemaphoreType.DMA((n_e,)),
        pltpu.SemaphoreType.DMA((n_e,)),
        pltpu.SemaphoreType.DMA((n_e,)),
        pltpu.SemaphoreType.DMA((n_e,)),
        pltpu.SemaphoreType.DMA((2,)),
        pltpu.SemaphoreType.DMA((2,)),
        pltpu.SemaphoreType.DMA((2,)),
        pltpu.SemaphoreType.DMA((2,)),
    ]
    anywhere = pl.BlockSpec(memory_space=pltpu.HBM)
    density = pl.pallas_call(
        kernel,
        out_shape=jax.ShapeDtypeStruct((2, 2, 2, width), full),
        in_specs=[anywhere] * 5 + [pl.BlockSpec(memory_space=pltpu.SMEM)],
        out_specs=pl.BlockSpec(memory_space=pltpu.VMEM),
        scratch_shapes=scratch,
        compiler_params=pltpu.CompilerParams(
            collective_id=0, has_side_effects=True, vmem_limit_bytes=48 * 2**20
        ),
    )(
        *[
            pltpu.with_memory_space_constraint(array, pltpu.HBM)
            for array in (
                green_window.reshape(4, 2, entries),
                screened.reshape(4, total, columns),
                retarded[:, :, 0],
                energy_order.reshape(1, total),
                jnp.asarray(phase_tables(total)),
            )
        ],
        window_start,
    )
    return density[:, :, :, None, :]


def solution(mesh):
    in_specs = (
        P(None, None, "energy", "rows", None),
        P(None, None, None, "rows", "energy"),
        P(None, "energy", "rows", None, None, None),
        P(),
        P("rows"),
    )
    out_specs = P(None, None, "energy", "rows", None)
    return jax.shard_map(shards, mesh=mesh, in_specs=in_specs, out_specs=out_specs, check_vma=False)
```

```python
import functools
import math

import jax
import jax.numpy as jnp
import numpy as np
from jax import lax
from jax.experimental import pallas as pl
from jax.experimental.pallas import tpu as pltpu
from jax.sharding import PartitionSpec as P

MESH = pl.DeviceIdType.MESH
PLANES = 8
LANES = 128


def phase_tables(total):
    turns = np.outer(np.arange(total), np.arange(total)) % total
    angle = 2.0 * math.pi / total * turns
    parts = []
    for exact in (np.cos(angle), np.sin(angle)):
        high = exact.astype(jnp.bfloat16)
        low = (exact - high.astype(np.float64)).astype(jnp.bfloat16)
        parts.append((high, low))
    stacked = np.stack([parts[0][0], parts[1][0], parts[0][1], parts[1][1]])
    return np.tile(stacked, (1, 1, 4))


def dot(left, right):
    return jnp.dot(left, right, preferred_element_type=jnp.float32)


def iota(shape, axis):
    return lax.broadcasted_iota(jnp.int32, shape, axis)


def kernel(
    green, screened, retarded, order, tables, start, out,
    green_v, screen_v, own_v, order_v, tables_v,
    flat, chunks, land_one, weights, forward, backward,
    chunks_two, land_two, rows_two, land_far, rows_far, far_v, from_left, from_right, right_side, spread, halo_out, halo_in,
    local_sem, send_one, recv_one, send_two, recv_two, send_far, recv_far, ret_send, ret_recv, halo_send, halo_recv,
):
    n_e = lax.axis_size("energy")
    n_r = lax.axis_size("rows")
    me = lax.axis_index("energy")
    row = lax.axis_index("rows")
    slab, width = own_v.shape[2], own_v.shape[3]
    total = order_v.shape[1]
    per = slab // n_e
    middle = n_r // 2
    far_row = 2 * middle - 1 - row
    far_side = middle - row
    is_far = jnp.logical_or(row == middle - 1, row == middle)
    has_left = jnp.logical_and(row > 0, row != middle)
    has_right = jnp.logical_and(row < n_r - 1, row != middle - 1)

    plane = max(1, n_e // PLANES)
    planes = n_e // plane

    def turned(step):
        turn = step // plane
        return turn + lax.rem(row, 2) * (1 - 2 * lax.rem(turn, 2))

    def far_first(step):
        turn = step // plane
        shift = planes // 2 + (turn + 1) // 2 * (1 - 2 * lax.rem(turn + row, 2))
        return lax.rem(me // plane + shift, planes) * plane + lax.rem(me + step, plane)

    barrier = pltpu.get_barrier_semaphore()

    @pl.loop(0, n_e)
    def _(step):
        other = far_first(step)

        @pl.when(other != me)
        def _():
            pl.semaphore_signal(barrier, inc=1, device_id={"energy": other}, device_id_type=MESH)

    @pl.when(row > 0)
    def _():
        pl.semaphore_signal(barrier, inc=1, device_id={"rows": row - 1}, device_id_type=MESH)

    @pl.when(row < n_r - 1)
    def _():
        pl.semaphore_signal(barrier, inc=1, device_id={"rows": row + 1}, device_id_type=MESH)

    halo_out[...] = jnp.zeros_like(halo_out)

    loads = [
        pltpu.make_async_copy(green, green_v, local_sem.at[0]),
        pltpu.make_async_copy(order, order_v, local_sem.at[1]),
        pltpu.make_async_copy(tables, tables_v, local_sem.at[2]),
        pltpu.make_async_copy(screened, screen_v, local_sem.at[3]),
        pltpu.make_async_copy(retarded.at[:, :, 1], own_v, local_sem.at[4]),
    ]
    for load in loads:
        load.start()
    far_load = pltpu.make_async_copy(retarded.at[:, :, 2 * far_side], far_v, local_sem.at[6])

    @pl.when(is_far)
    def _():
        far_load.start()

    loads[0].wait()
    for pair in range(4):
        flat[2 * pair : 2 * pair + 2, :] = green_v[pair].astype(jnp.float32)
    group = n_e
    for size in (1, 2, 4, 8, 16):
        if size < n_e and n_e % size == 0 and size * per * slab % LANES == 0:
            group = size
            break
    margin = jnp.zeros((8, LANES - slab), jnp.float32)

    @pl.loop(0, n_e // group)
    def _(step):
        window = group * per * slab
        if group == n_e:
            cut = flat[...]
        else:
            cut = flat[:, pl.ds(pl.multiple_of(step * window, LANES), window)]
        for place in range(group * per):
            piece = cut[:, place * slab : (place + 1) * slab]
            lane = place % per * LANES
            chunks[step * group + place // per, :, lane : lane + LANES] = jnp.concatenate(
                [piece, margin], axis=1
            ).astype(jnp.bfloat16)

    beside = (row + n_r - 1) // n_r + (2 * n_r - 2 - row) // n_r
    pl.semaphore_wait(barrier, n_e - 1 + beside)

    def exchange(source, target, send_sem, recv_sem, other):
        return pltpu.make_async_remote_copy(
            src_ref=source.at[other],
            dst_ref=target.at[me],
            send_sem=send_sem.at[other],
            recv_sem=recv_sem.at[me],
            device_id={"energy": other},
            device_id_type=MESH,
        )

    def arrival(source, target, send_sem, recv_sem, other):
        return pltpu.make_async_remote_copy(
            src_ref=source.at[other],
            dst_ref=target.at[other],
            send_sem=send_sem.at[other],
            recv_sem=recv_sem.at[other],
            device_id={"energy": other},
            device_id_type=MESH,
        )

    def cross(step, device):
        return pltpu.make_async_remote_copy(
            src_ref=chunks_two.at[step],
            dst_ref=land_far.at[device],
            send_sem=send_far.at[step],
            recv_sem=recv_far.at[device],
            device_id={"energy": step, "rows": far_row},
            device_id_type=MESH,
        )

    one = (chunks, land_one, send_one, recv_one)
    two = (chunks_two, land_two, send_two, recv_two)

    @pl.loop(0, n_e)
    def _(step):
        other = far_first(step)

        @pl.when(other != me)
        def _():
            exchange(*one, other).start()

    to_right = pltpu.make_async_remote_copy(
        src_ref=retarded.at[:, :, 2], dst_ref=from_left, send_sem=ret_send.at[0], recv_sem=ret_recv.at[0],
        device_id={"rows": lax.rem(row + 1, n_r)}, device_id_type=MESH,
    )
    to_left = pltpu.make_async_remote_copy(
        src_ref=retarded.at[:, :, 0], dst_ref=from_right, send_sem=ret_send.at[1], recv_sem=ret_recv.at[1],
        device_id={"rows": lax.rem(row + n_r - 1, n_r)}, device_id_type=MESH,
    )

    @pl.when(has_right)
    def _():
        to_right.start()

    @pl.when(has_left)
    def _():
        to_left.start()

    land_one[me] = chunks[me]

    loads[1].wait()
    loads[2].wait()
    count = 4 * total
    energies = (iota((total, total), 0) == order_v[...]).astype(jnp.bfloat16)
    column = iota((total, count), 1)
    slot_of_column = column // 8 * 2 + column % 2
    pick = (iota((total, count), 0) == slot_of_column).astype(jnp.bfloat16)
    hot = dot(energies, pick).astype(jnp.bfloat16)
    shape = (total, count)
    col = iota(shape, 1)
    col_g, col_c = col // 4 % 2, col // 2 % 2
    for part in range(2):
        cosine = dot(tables_v[2 * part, :, :total], hot)
        sine = dot(tables_v[2 * part + 1, :, :total], hot)
        for g in range(2):
            real = jnp.where(col_c == 0, cosine, sine)
            imag = jnp.where(col_c == 0, -sine, cosine)
            base = part * count + g * 2 * total
            forward[base : base + total, :] = jnp.where(col_g == g, real, 0.0).astype(jnp.bfloat16)
            forward[base + total : base + 2 * total, :] = jnp.where(col_g == g, imag, 0.0).astype(jnp.bfloat16)
    half = 2 * total
    line = iota((half, total), 0)
    slot_of_line = line // 4 * 2 + line % 2
    pick_line = (iota((half, total), 1) == slot_of_line).astype(jnp.bfloat16)
    hot_line = lax.dot_general(
        pick_line, energies, (((1,), (1,)), ((), ())), preferred_element_type=jnp.float32
    ).astype(jnp.bfloat16)
    shape = (half, count)
    same_g = iota(shape, 0) // 2 % 2 == iota(shape, 1) // (2 * total)
    from_real = iota(shape, 1) // total % 2 == 0
    scale = 1.0 / total
    for part in range(2):
        cosine = dot(hot_line, tables_v[2 * part]) * scale
        sine = dot(hot_line, tables_v[2 * part + 1]) * scale
        real = jnp.where(from_real, -sine, -cosine)
        imag = jnp.where(from_real, cosine, -sine)
        base = part * count
        backward[base : base + half, :] = jnp.where(same_g, real, 0.0).astype(jnp.bfloat16)
        backward[base + half : base + count, :] = jnp.where(same_g, imag, 0.0).astype(jnp.bfloat16)

    loads[3].wait()
    screen_margin = jnp.zeros((total, LANES - slab), jnp.float32)
    for pair in range(4):
        entries = screen_v[pair].astype(jnp.float32)
        for p in range(per):
            weights[pair * total : (pair + 1) * total, p * LANES : (p + 1) * LANES] = jnp.concatenate(
                [entries[:, p * slab : (p + 1) * slab], screen_margin], axis=1
            )

    lines = 4 * n_e
    line = iota((lines, slab), 0)
    orbital = iota((lines, slab), 1)
    blank = jnp.zeros((LANES - slab, width), jnp.bfloat16)

    def prepare(block, target):
        for slot in range(2):
            real = block[0, slot]
            imag = block[1, slot]
            for side, (upper, lower) in enumerate(((real, imag), (-imag, real))):
                right_side[target, slot, side, 0:slab] = upper
                right_side[target, slot, side, slab:LANES] = blank
                right_side[target, slot, side, LANES : LANES + slab] = lower
                right_side[target, slot, side, LANES + slab :] = blank
            for p in range(per):
                chosen = jnp.where(line % 2 == slot, line // 4 * per + p, -1)
                select = (orbital == chosen).astype(jnp.bfloat16)
                for part, values in enumerate((real, imag)):
                    rows = dot(select, values)
                    spread[target, part, p] = rows if slot == 0 else spread[target, part, p] + rows

    loads[4].wait()
    prepare(own_v, 2)

    @pl.when(is_far)
    def _():
        far_load.wait()
        prepare(far_v, far_side)

    @pl.loop(1, n_e)
    def _(step):
        arrival(*one, lax.rem(me + step, n_e)).wait_recv()

    arrived = land_one[...].reshape(8 * n_e, per * LANES)
    times = dot(forward[...], arrived)
    times = times[:count] + times[count:]
    mixed = []
    for g in range(2):
        base = g * 2 * total
        green_re, green_im = times[base : base + total], times[base + total : base + 2 * total]
        screen_re, screen_im = weights[base : base + total], weights[base + total : base + 2 * total]
        mixed.append(green_re * screen_re - green_im * screen_im)
        mixed.append(green_re * screen_im + green_im * screen_re)
    mixed = jnp.concatenate(mixed, axis=0)
    high = mixed.astype(jnp.bfloat16)
    low = (mixed - high.astype(jnp.float32)).astype(jnp.bfloat16)
    first = dot(backward[...], high)
    sigma = first[:count] + (first[count:] + dot(backward[0:count], low))
    sigma = sigma.astype(jnp.bfloat16)
    for c in range(2):
        for p in range(per):
            lane = (2 * p + c) * LANES
            chunks_two[:, :, lane : lane + LANES] = sigma[
                c * half : (c + 1) * half, p * LANES : (p + 1) * LANES
            ].reshape(n_e, 4, LANES)

    @pl.loop(0, n_e)
    def _(step):
        other = turned(step) * plane + lax.rem(me + step, plane)

        @pl.when(other != me)
        def _():
            exchange(*two, other).start()

    @pl.when(is_far)
    def _():
        @pl.loop(0, n_e)
        def _(step):
            cross(turned(step) * plane + lax.rem(me + step, plane), me).start()

    land_two[me] = chunks_two[me]

    @pl.when(has_left)
    def _():
        to_right.wait_recv()
        prepare(from_left, 0)

    @pl.when(has_right)
    def _():
        to_left.wait_recv()
        prepare(from_right, 1)

    @pl.loop(1, n_e)
    def _(step):
        exchange(*one, lax.rem(me + step, n_e)).wait_send()

    @pl.loop(1, n_e)
    def _(step):
        arrival(*two, lax.rem(me + step, n_e)).wait_recv()

    def regroup(landed, grouped):
        for p in range(per):
            grouped[p] = landed[:, :, 2 * p * LANES : 2 * (p + 1) * LANES].reshape(lines, 2 * LANES)

    regroup(land_two, rows_two)

    def fold(values):
        values = values.reshape(lines // 8, 8, values.shape[1]).sum(axis=0)
        return values[0:4] + values[4:8]

    first_slot = iota((lines, width), 0) % 2 == 0

    def contribution(target, grouped):
        real = jnp.zeros((4, width), jnp.float32)
        imag = jnp.zeros((4, width), jnp.float32)
        for p in range(per):
            inner_re, inner_im = (
                jnp.where(
                    first_slot,
                    dot(grouped[p], right_side[target, 0, side]),
                    dot(grouped[p], right_side[target, 1, side]),
                )
                for side in range(2)
            )
            outer_re = spread[target, 0, p]
            outer_im = spread[target, 1, p]
            real = real + fold(outer_re * inner_re - outer_im * inner_im)
            imag = imag + fold(outer_re * inner_im + outer_im * inner_re)
        return jnp.concatenate([real, imag], axis=0)

    def give(side):
        return pltpu.make_async_remote_copy(
            src_ref=halo_out.at[side],
            dst_ref=halo_in.at[1 - side],
            send_sem=halo_send.at[side],
            recv_sem=halo_recv.at[1 - side],
            device_id={"rows": lax.rem(row + n_r - 1 + 2 * side, n_r)},
            device_id_type=MESH,
        )

    @pl.when(jnp.logical_not(has_left))
    def _():
        halo_in[0] = jnp.zeros(halo_in.shape[1:], jnp.float32)

    @pl.when(jnp.logical_not(has_right))
    def _():
        halo_in[1] = jnp.zeros(halo_in.shape[1:], jnp.float32)

    @pl.loop(0, 2)
    def _(turn):
        side = lax.rem(row + turn, 2)

        @pl.when(jnp.logical_or(jnp.logical_and(side == 0, has_left), jnp.logical_and(side == 1, has_right)))
        def _():
            halo_out[side, :, :width] = contribution(side, rows_two)
            give(side).start()

    density = contribution(2, rows_two)
    direct = [jnp.zeros((4, LANES), jnp.float32), jnp.zeros((4, LANES), jnp.float32)]
    shape = (lines, LANES)
    for p in range(per):
        on_diagonal = iota(shape, 1) == iota(shape, 0) // 4 * per + p
        for c in range(2):
            entries = rows_two[p, :, c * LANES : (c + 1) * LANES].astype(jnp.float32)
            direct[c] = direct[c] + fold(jnp.where(on_diagonal, entries, 0.0))
    shape = (LANES, width)
    place = iota(shape, 1) == iota(shape, 0) + start[0]
    density = density + dot(
        jnp.concatenate(direct, axis=0).astype(jnp.bfloat16), place.astype(jnp.bfloat16)
    )

    @pl.when(is_far)
    def _():
        @pl.loop(0, n_e)
        def _(step):
            cross(step, step).wait_recv()

        regroup(land_far, rows_far)
        halo_in[far_side, :, :width] = contribution(far_side, rows_far)

    @pl.loop(1, n_e)
    def _(step):
        exchange(*two, lax.rem(me + step, n_e)).wait_send()

    @pl.when(is_far)
    def _():
        @pl.loop(0, n_e)
        def _(step):
            cross(step, me).wait_send()

    @pl.when(has_right)
    def _():
        to_right.wait_send()
        give(1).wait_send()

    @pl.when(has_left)
    def _():
        to_left.wait_send()
        give(0).wait_send()

    @pl.when(has_left)
    def _():
        give(1).wait_recv()

    @pl.when(has_right)
    def _():
        give(0).wait_recv()

    density = density + halo_in[0, :, :width] + halo_in[1, :, :width]
    for c in range(2):
        for g in range(2):
            out[g, c] = density[4 * c + 2 * g : 4 * c + 2 * g + 2]


def shards(green_window, screened, retarded, energy_order, window_start):
    n_e = lax.axis_size("energy")
    entries = green_window.shape[4]
    columns = screened.shape[4]
    total = screened.shape[2]
    slab, width = retarded.shape[4], retarded.shape[5]
    per = slab // n_e
    half = jnp.bfloat16
    full = jnp.float32
    lines = 4 * n_e
    padded = pl.cdiv(width, LANES) * LANES
    scratch = [
        pltpu.VMEM((4, 2, entries), half),
        pltpu.VMEM((4, total, columns), half),
        pltpu.VMEM((2, 2, slab, width), half),
        pltpu.VMEM((1, total), jnp.int32),
        pltpu.VMEM((4, total, 4 * total), half),
        pltpu.VMEM((8, entries), full),
        pltpu.VMEM((n_e, 8, per * LANES), half),
        pltpu.VMEM((n_e, 8, per * LANES), half),
        pltpu.VMEM((4 * total, per * LANES), full),
        pltpu.VMEM((8 * total, 4 * total), half),
        pltpu.VMEM((8 * total, 4 * total), half),
        pltpu.VMEM((n_e, 4, 2 * per * LANES), half),
        pltpu.VMEM((n_e, 4, 2 * per * LANES), half),
        pltpu.VMEM((per, lines, 2 * LANES), half),
        pltpu.VMEM((n_e, 4, 2 * per * LANES), half),
        pltpu.VMEM((per, lines, 2 * LANES), half),
        pltpu.VMEM((2, 2, slab, width), half),
        pltpu.VMEM((2, 2, slab, width), half),
        pltpu.VMEM((2, 2, slab, width), half),
        pltpu.VMEM((3, 2, 2, 2 * LANES, width), half),
        pltpu.VMEM((3, 2, per, lines, width), full),
        pltpu.VMEM((2, 8, padded), full),
        pltpu.VMEM((2, 8, padded), full),
        pltpu.SemaphoreType.DMA((7,)),
        pltpu.SemaphoreType.DMA((n_e,)),
        pltpu.SemaphoreType.DMA((n_e,)),
        pltpu.SemaphoreType.DMA((n_e,)),
        pltpu.SemaphoreType.DMA((n_e,)),
        pltpu.SemaphoreType.DMA((n_e,)),
        pltpu.SemaphoreType.DMA((n_e,)),
        pltpu.SemaphoreType.DMA((2,)),
        pltpu.SemaphoreType.DMA((2,)),
        pltpu.SemaphoreType.DMA((2,)),
        pltpu.SemaphoreType.DMA((2,)),
    ]
    anywhere = pl.BlockSpec(memory_space=pltpu.HBM)
    density = pl.pallas_call(
        kernel,
        out_shape=jax.ShapeDtypeStruct((2, 2, 2, width), full),
        in_specs=[anywhere] * 5 + [pl.BlockSpec(memory_space=pltpu.SMEM)],
        out_specs=pl.BlockSpec(memory_space=pltpu.VMEM),
        scratch_shapes=scratch,
        compiler_params=pltpu.CompilerParams(
            collective_id=0, has_side_effects=True, vmem_limit_bytes=48 * 2**20
        ),
    )(
        *[
            pltpu.with_memory_space_constraint(array, pltpu.HBM)
            for array in (
                green_window.reshape(4, 2, entries),
                screened.reshape(4, total, columns),
                retarded[:, :, 0],
                energy_order.reshape(1, total),
                jnp.asarray(phase_tables(total)),
            )
        ],
        window_start,
    )
    return density[:, :, :, None, :]


def solution(mesh):
    in_specs = (
        P(None, None, "energy", "rows", None),
        P(None, None, None, "rows", "energy"),
        P(None, "energy", "rows", None, None, None),
        P(),
        P("rows"),
    )
    out_specs = P(None, None, "energy", "rows", None)
    return jax.shard_map(shards, mesh=mesh, in_specs=in_specs, out_specs=out_specs, check_vma=False)
```
